128 devices in a mesh: tm: 16 (over x_hi, y, core), input: 8 (over x_lo, z).
Axes of the slice: x: 4 (x_hi: 2, x_lo: 2; x = x_hi * 2 + x_lo), y: 4, z: 4, core: 2. Of those that a mesh axis runs over, the one named last changes fastest.
Arguments:
- samples: int32 [1024, 262144], P('input', 'tm'), may hold values from -16 to 16, as said below
- coefficients: float32 [8, 512], replicated, may hold values from -2 to 2
Outputs:
- visibility: bfloat16 [256, 2, 1024, 1024], P(('tm', 'input'))
The draws below stay inside these ranges and needn't reach their ends.
Inputs may be any that keep to these rules, and one draw needn't show every extreme that they name: `samples`: noise-dominated integer voltages: each input carries independent integer noise plus a weak common signal.
All inputs are finite; a program needn't handle non-finite values.
Results may differ from the reference program's by a relative error of at most 0.007.
Values may be sent and summed in bfloat16 or wider, within the bound.
No kernel may reach another device: no remote copies, remote signals or barrier semaphores. Data moves between devices by JAX's collectives and lax.ppermute only.
A program may use at most 128 MiB of HBM per device.

```python
import math
import jax
import jax.numpy as jnp
from jax import lax

INPUTS = 1024
NFFT = 512
TAPS = 8
FRAMES = 512
CHANNELS = 256


def draw_samples(key, part):
    keys_all = jax.random.split(key, 4)
    total_len = FRAMES * NFFT
    sky_signal = jax.random.randint(keys_all[0], (total_len + 64,), -2, 3)
    delays = jax.random.randint(keys_all[1], (INPUTS,), 0, 64)
    gains = jax.random.randint(keys_all[2], (INPUTS, 1), 1, 3)
    noise_part = jax.random.randint(keys_all[3], (INPUTS, total_len), -12, 13)

    def shift_row(delay_value):
        return lax.dynamic_slice_in_dim(sky_signal, delay_value, total_len)
    shifted = jax.vmap(shift_row)(delays)
    result_samples = gains * shifted + noise_part
    result_samples = result_samples.at[0, 0].set(16).at[0, 1].set(-16)
    return result_samples.astype(jnp.int32)


def gaussian(own_key, dims, scale, limit, held_as=jnp.bfloat16):
    result = jax.random.normal(own_key, dims, jnp.float32) * scale
    return jnp.minimum(jnp.maximum(result, -limit), limit).astype(held_as)


def setup_inputs(seed: int = 0) -> dict:
    keys = jax.random.split(jax.random.key(seed), 3)
    return {
        "samples": draw_samples(jax.random.fold_in(keys[2], 71), 0),
        "coefficients": gaussian(keys[1], (TAPS, NFFT), TAPS ** -0.5, 2.0, jnp.float32),
    }


def dft_table(length):
    row_index = jnp.arange(length, dtype=jnp.int32)
    channel = row_index // 2
    parity = row_index % 2
    positions = jnp.arange(length, dtype=jnp.int32)
    phase_index = channel[:, None] * positions[None, :] % length
    angles = phase_index.astype(jnp.float32) * (2.0 * math.pi / length)
    values = jnp.where(parity[:, None] == 0, jnp.cos(angles), -jnp.sin(angles)) / math.sqrt(length)
    return values.astype(jnp.bfloat16)

def reference(samples, coefficients):
    signal = samples.astype(jnp.float32) / 8.0
    framed = signal.reshape(INPUTS, FRAMES, NFFT)
    padded = jnp.concatenate([jnp.zeros((INPUTS, TAPS - 1, NFFT), jnp.float32), framed], axis=1)
    filtered = jnp.zeros((INPUTS, FRAMES, NFFT), jnp.float32)
    for tap_index in range(TAPS):
        start_frame = TAPS - 1 - tap_index
        filtered = filtered + coefficients[tap_index][None, None, :] * padded[:, start_frame:start_frame + FRAMES, :]
    filtered = filtered.astype(jnp.bfloat16)
    spectra = jnp.dot(filtered.reshape(INPUTS * FRAMES, NFFT), dft_table(NFFT).T, preferred_element_type=jnp.float32).astype(jnp.bfloat16)
    spectra = spectra.reshape(INPUTS, FRAMES, CHANNELS, 2).transpose(2, 3, 1, 0)

    def correlate_one(channel_block):
        stacked = channel_block.reshape(2 * FRAMES, INPUTS).astype(jnp.float32)
        real_part = jnp.dot(stacked.T, stacked, preferred_element_type=jnp.float32)
        cross_part = jnp.dot(channel_block[1].astype(jnp.float32).T, channel_block[0].astype(jnp.float32), preferred_element_type=jnp.float32)
        imag_part = cross_part - cross_part.T
        return (jnp.stack([real_part, imag_part]) / FRAMES).astype(jnp.bfloat16)
    return lax.map(correlate_one, spectra)
```

```python
import functools

import jax
import jax.numpy as jnp
import ml_dtypes
import numpy as np
from jax import lax
from jax.experimental import pallas as pl
from jax.experimental.pallas import tpu as pltpu
from jax.sharding import PartitionSpec as P

GROUP = 8
BLOCK = 256


def dft_table(length):
    channel = np.arange(length) // 2
    phase = channel[:, None] * np.arange(length)[None, :] % length
    angles = phase * (2.0 * np.pi / length)
    real = (np.arange(length) % 2 == 0)[:, None]
    values = np.where(real, np.cos(angles), -np.sin(angles)) / np.sqrt(length)
    return values.astype(ml_dtypes.bfloat16)


def filter_group(cur_ref, tail, coef_ref, table_ref, out_ref, filt, spread):
    taps, fft = coef_ref.shape
    inputs = cur_ref.shape[0]
    past = taps - 1

    def rows_step(it, carry):
        rows = pl.ds(pl.multiple_of(it * 16, 16), 16)
        for n0 in range(0, fft, 128):
            coefs = [coef_ref[p : p + 1, n0 : n0 + 128] for p in range(taps)]
            window = [tail[rows, k * fft + n0 : k * fft + n0 + 128] for k in range(past)]
            for f in range(GROUP):
                window.append(cur_ref[rows, f * fft + n0 : f * fft + n0 + 128].astype(jnp.float32))
                total = coefs[0] * window[-1]
                for p in range(1, taps):
                    total = total + coefs[p] * window[-1 - p]
                filt[f, rows, n0 : n0 + 128] = total.astype(jnp.bfloat16)
                window.pop(0)
        return carry

    lax.fori_loop(0, inputs // 16, rows_step, 0)
    for f in range(0, GROUP, 2):
        pair = filt[f : f + 2].reshape(2 * inputs, fft)
        spectra = lax.dot_general(
            table_ref[...], pair, (((1,), (1,)), ((), ())), preferred_element_type=jnp.float32
        )
        spread[pl.ds(f, fft, stride=GROUP), :] = spectra[:, :inputs]
        spread[pl.ds(f + 1, fft, stride=GROUP), :] = spectra[:, inputs:]
    out_ref[...] = spread[...].reshape(fft, GROUP, inputs).astype(jnp.bfloat16)


def later_kernel(first_ref, cur_ref, coef_ref, table_ref, out_ref, tail, filt, spread):
    fft = coef_ref.shape[1]

    @pl.when(pl.program_id(0) == 0)
    def _():
        tail[...] = first_ref[:, fft:].astype(jnp.float32)

    filter_group(cur_ref, tail, coef_ref, table_ref, out_ref, filt, spread)
    tail[...] = cur_ref[:, fft:].astype(jnp.float32)


def first_kernel(halo_ref, cur_ref, coef_ref, table_ref, _, out_ref, tail, filt, spread):
    tail[...] = halo_ref[...].astype(jnp.float32)
    filter_group(cur_ref, tail, coef_ref, table_ref, out_ref, filt, spread)


def correlate_kernel(recv_ref, out_ref, held, turned, swapped):
    tm_count, input_count, _, _, frames, inputs = recv_ref.shape
    half = tm_count * frames
    width = input_count * inputs
    for r in range(2):
        for a in range(tm_count):
            for b in range(input_count):
                rows = slice(r * half + a * frames, r * half + (a + 1) * frames)
                cols = slice(b * inputs, (b + 1) * inputs)
                held[rows, cols] = recv_ref[a, b, 0, r]
    turned[...] = held[...].T
    swapped[:half] = -held[half:]
    swapped[half:] = held[:half]
    scale = 1.0 / half
    for i in range(0, width, BLOCK):
        for j in range(i, width, BLOCK):
            left = turned[i : i + BLOCK]
            real = jnp.dot(left, held[:, j : j + BLOCK], preferred_element_type=jnp.float32) * scale
            imag = jnp.dot(left, swapped[:, j : j + BLOCK], preferred_element_type=jnp.float32) * scale
            out_ref[0, 0, i : i + BLOCK, j : j + BLOCK] = real.astype(jnp.bfloat16)
            out_ref[0, 1, i : i + BLOCK, j : j + BLOCK] = imag.astype(jnp.bfloat16)
            if j > i:
                out_ref[0, 0, j : j + BLOCK, i : i + BLOCK] = real.T.astype(jnp.bfloat16)
                out_ref[0, 1, j : j + BLOCK, i : i + BLOCK] = (-imag.T).astype(jnp.bfloat16)


def local(samples, coefficients):
    inputs, sample_count = samples.shape
    taps, fft = coefficients.shape
    frames = sample_count // fft
    tm_count = lax.axis_size("tm")
    input_count = lax.axis_size("input")
    devices = tm_count * input_count
    groups = frames // GROUP
    span = GROUP * fft
    past = (taps - 1) * fft
    table = jnp.asarray(dft_table(fft))

    tail = samples[:, sample_count - past :].astype(jnp.bfloat16)
    route = [(i - 1, i) for i in range(1, tm_count)]
    halo = lax.ppermute(tail, "tm", route)
    scaled = coefficients * 0.125

    whole = lambda *shape: pl.BlockSpec(shape, lambda g: (0,) * len(shape))
    scratch = [
        pltpu.VMEM((inputs, past), jnp.float32),
        pltpu.VMEM((GROUP, inputs, fft), jnp.bfloat16),
        pltpu.VMEM((fft * GROUP, inputs), jnp.float32),
    ]
    shape = jax.ShapeDtypeStruct((fft, frames, inputs), jnp.bfloat16)
    spectra = pl.pallas_call(
        later_kernel,
        grid=(groups - 1,),
        in_specs=[
            whole(inputs, span),
            pl.BlockSpec((inputs, span), lambda g: (0, g + 1)),
            whole(taps, fft),
            whole(fft, fft),
        ],
        out_specs=pl.BlockSpec((fft, GROUP, inputs), lambda g: (0, g + 1, 0)),
        out_shape=shape,
        scratch_shapes=scratch,
        name="later_frames",
    )(samples, samples, scaled, table)
    spectra = pl.pallas_call(
        first_kernel,
        grid=(1,),
        in_specs=[
            whole(inputs, past),
            whole(inputs, span),
            whole(taps, fft),
            whole(fft, fft),
            pl.BlockSpec(memory_space=pl.ANY),
        ],
        out_specs=pl.BlockSpec((fft, GROUP, inputs), lambda g: (0, 0, 0)),
        out_shape=shape,
        scratch_shapes=scratch,
        input_output_aliases={4: 0},
        name="first_frames",
    )(halo, samples, scaled, table, spectra)

    items = fft // (2 * devices)
    outgoing = spectra.reshape(devices, 2 * items, frames, inputs)
    received = lax.all_to_all(outgoing, ("tm", "input"), 0, 0, tiled=True)
    received = received.reshape(tm_count, input_count, items, 2, frames, inputs)
    depth = 2 * tm_count * frames
    width = input_count * inputs
    return pl.pallas_call(
        correlate_kernel,
        grid=(items,),
        in_specs=[
            pl.BlockSpec(
                (tm_count, input_count, 1, 2, frames, inputs), lambda c: (0, 0, c, 0, 0, 0)
            )
        ],
        out_specs=pl.BlockSpec((1, 2, width, width), lambda c: (c, 0, 0, 0)),
        out_shape=jax.ShapeDtypeStruct((items, 2, width, width), jnp.bfloat16),
        scratch_shapes=[
            pltpu.VMEM((depth, width), jnp.bfloat16),
            pltpu.VMEM((width, depth), jnp.bfloat16),
            pltpu.VMEM((depth, width), jnp.bfloat16),
        ],
        name="correlate",
    )(received)


def solution(mesh):
    in_specs = (P("input", "tm"), P())
    out_specs = P(("tm", "input"), None, None, None)
    return jax.shard_map(local, mesh=mesh, in_specs=in_specs, out_specs=out_specs, check_vma=False)
```

```python
import jax
import jax.numpy as jnp
import ml_dtypes
import numpy as np
from jax import lax
from jax.experimental import pallas as pl
from jax.experimental.pallas import tpu as pltpu
from jax.sharding import PartitionSpec as P

GROUP = 8
BLOCK = 256
ROWS = 16
LANES = 128


def dft_table(length):
    channel = np.arange(length) // 2
    phase = channel[:, None] * np.arange(length)[None, :] % length
    angles = phase * (2.0 * np.pi / length)
    real = (np.arange(length) % 2 == 0)[:, None]
    values = np.where(real, np.cos(angles), -np.sin(angles)) / np.sqrt(length)
    return (values.astype(ml_dtypes.bfloat16).astype(np.float32) / 8.0).astype(ml_dtypes.bfloat16)


def transform(filt, table_ref, spread, stage, spectra_ref, group, sem):
    frames, inputs, fft = filt.shape
    for f in range(0, frames, 2):
        pair = filt[f : f + 2].reshape(2 * inputs, fft)
        spectra = lax.dot_general(
            table_ref[...], pair, (((1,), (1,)), ((), ())), preferred_element_type=jnp.float32
        )
        spread[pl.ds(f, fft, stride=frames), :] = spectra[:, :inputs]
        spread[pl.ds(f + 1, fft, stride=frames), :] = spectra[:, inputs:]
    block = spread[...].reshape(fft, frames, inputs).astype(jnp.bfloat16)
    stage[...] = block
    copy = pltpu.make_async_copy(
        stage, spectra_ref.at[:, pl.ds(group * frames, frames), :], sem
    )
    copy.start()
    return copy


def own_kernel(
    samples_ref, coef_hbm, table_hbm, spectra_ref, partial_ref,
    coef_ref, table_ref, held, filt, spread, stage, sems, out_sems,
):
    taps, fft = coef_ref.shape
    groups, inputs, span = held.shape
    coef_copy = pltpu.make_async_copy(coef_hbm, coef_ref, sems.at[groups])
    coef_copy.start()
    copies = []
    for g in range(groups):
        copy = pltpu.make_async_copy(
            samples_ref.at[:, pl.ds(g * span, span)], held.at[g], sems.at[g]
        )
        copy.start()
        copies.append(copy)
    table_copy = pltpu.make_async_copy(table_hbm, table_ref, sems.at[groups + 1])
    table_copy.start()
    coef_copy.wait()
    results = []

    for g in range(groups):
        copies[g].wait()

        def rows_step(it, carry, g=g):
            rows = pl.ds(pl.multiple_of(it * ROWS, ROWS), ROWS)
            for n0 in range(0, fft, LANES):
                coefs = [coef_ref[p : p + 1, n0 : n0 + LANES] for p in range(taps)]

                def frame(f):
                    where, k = (g, f) if f >= 0 else (g - 1, f + GROUP)
                    return held[where, rows, k * fft + n0 : k * fft + n0 + LANES].astype(jnp.float32)

                window = [frame(f) for f in range(1 - taps, 0)] if g else []
                for f in range(GROUP):
                    window.append(frame(f))
                    total = coefs[0] * window[-1]
                    for p in range(1, min(taps, len(window))):
                        total = total + coefs[p] * window[-1 - p]
                    if g:
                        filt[f, rows, n0 : n0 + LANES] = total.astype(jnp.bfloat16)
                    else:
                        partial_ref[f, rows, n0 : n0 + LANES] = total
                    if len(window) == taps:
                        window.pop(0)
            return carry

        lax.fori_loop(0, inputs // ROWS, rows_step, 0)
        if g:
            if g == 1:
                table_copy.wait()
            results.append(
                transform(filt, table_ref, spread, stage.at[g - 1], spectra_ref, g, out_sems.at[g - 1])
            )
    for copy in results:
        copy.wait()


def first_kernel(
    flag_ref, halo_ref, partial_ref, coef_ref, table_ref, _, spectra_ref, filt, spread, stage, sem
):
    taps, fft = coef_ref.shape
    inputs = halo_ref.shape[0]
    past = taps - 1
    flag = flag_ref[0]

    def rows_step(it, carry):
        rows = pl.ds(pl.multiple_of(it * ROWS, ROWS), ROWS)
        for n0 in range(0, fft, LANES):
            coefs = [coef_ref[p : p + 1, n0 : n0 + LANES] * flag for p in range(taps)]
            window = [
                halo_ref[rows, k * fft + n0 : k * fft + n0 + LANES].astype(jnp.float32)
                for k in range(past)
            ]
            for f in range(GROUP):
                total = partial_ref[f, rows, n0 : n0 + LANES]
                for p in range(f + 1, taps):
                    total = total + coefs[p] * window[f - p + past]
                filt[f, rows, n0 : n0 + LANES] = total.astype(jnp.bfloat16)
        return carry

    lax.fori_loop(0, inputs // ROWS, rows_step, 0)
    transform(filt, table_ref, spread, stage, spectra_ref, 0, sem).wait()


def correlate_kernel(recv_ref, out_ref, held, turned, swapped, stage, sems):
    tm_count, input_count, items, _, frames, inputs = recv_ref.shape
    half = tm_count * frames
    width = input_count * inputs
    scale = 1.0 / half
    copies = []

    def give(c, part, i, j, value):
        rows, cols = pl.ds(i, BLOCK), pl.ds(j, BLOCK)
        stage[c, part, rows, cols] = value.astype(jnp.bfloat16)
        copy = pltpu.make_async_copy(
            stage.at[c, part, rows, cols], out_ref.at[c, part, rows, cols], sems.at[len(copies)]
        )
        copy.start()
        copies.append(copy)

    for c in range(items):
        for r in range(2):
            for a in range(tm_count):
                for b in range(input_count):
                    rows = slice(r * half + a * frames, r * half + (a + 1) * frames)
                    cols = slice(b * inputs, (b + 1) * inputs)
                    held[c, rows, cols] = recv_ref[a, b, c, r]
        turned[c] = held[c].T
        swapped[c, :half] = -held[c, half:]
        swapped[c, half:] = held[c, :half]
        for i in range(0, width, BLOCK):
            for j in range(i, width, BLOCK):
                left = turned[c, i : i + BLOCK]
                real = scale * jnp.dot(
                    left, held[c, :, j : j + BLOCK], preferred_element_type=jnp.float32
                )
                imag = scale * jnp.dot(
                    left, swapped[c, :, j : j + BLOCK], preferred_element_type=jnp.float32
                )
                give(c, 0, i, j, real)
                give(c, 1, i, j, imag)
                if j > i:
                    give(c, 0, j, i, real.T)
                    give(c, 1, j, i, -imag.T)
    for copy in copies:
        copy.wait()


def local(samples, coefficients):
    inputs, sample_count = samples.shape
    taps, fft = coefficients.shape
    frames = sample_count // fft
    tm_count = lax.axis_size("tm")
    input_count = lax.axis_size("input")
    devices = tm_count * input_count
    groups = frames // GROUP
    past = (taps - 1) * fft
    table = jnp.asarray(dft_table(fft))
    vmem = pl.BlockSpec(memory_space=pltpu.VMEM)
    hbm = pl.BlockSpec(memory_space=pltpu.HBM)

    tail = samples[:, sample_count - past :].astype(jnp.bfloat16)
    route = [(i, (i + 1) % tm_count) for i in range(tm_count)]
    halo = lax.ppermute(tail, "tm", route)
    flag = jnp.where(lax.axis_index("tm") > 0, 1.0, 0.0).astype(jnp.float32).reshape(1)

    spectra_type = pltpu.HBM((fft, frames, inputs), jnp.bfloat16)
    in_hbm = lambda array: pltpu.with_memory_space_constraint(array, pltpu.HBM)
    filt = pltpu.VMEM((GROUP, inputs, fft), jnp.bfloat16)
    spread = pltpu.VMEM((fft * GROUP, inputs), jnp.float32)
    spectra, partial = pl.pallas_call(
        own_kernel,
        in_specs=[hbm, hbm, hbm],
        out_specs=[hbm, vmem],
        out_shape=[spectra_type, pltpu.VMEM((GROUP, inputs, fft), jnp.float32)],
        scratch_shapes=[
            pltpu.VMEM((taps, fft), jnp.float32),
            pltpu.VMEM((fft, fft), jnp.bfloat16),
            pltpu.VMEM((groups, inputs, GROUP * fft), jnp.int32),
            filt,
            spread,
            pltpu.VMEM((groups - 1, fft, GROUP, inputs), jnp.bfloat16),
            pltpu.SemaphoreType.DMA((groups + 2,)),
            pltpu.SemaphoreType.DMA((groups - 1,)),
        ],
        compiler_params=pltpu.CompilerParams(vmem_limit_bytes=24 << 20),
        name="own_frames",
    )(in_hbm(samples), in_hbm(coefficients), in_hbm(table))
    spectra = pl.pallas_call(
        first_kernel,
        in_specs=[pl.BlockSpec(memory_space=pltpu.SMEM)] + [vmem] * 4 + [hbm],
        out_specs=hbm,
        out_shape=spectra_type,
        scratch_shapes=[
            filt,
            spread,
            pltpu.VMEM((fft, GROUP, inputs), jnp.bfloat16),
            pltpu.SemaphoreType.DMA,
        ],
        input_output_aliases={5: 0},
        compiler_params=pltpu.CompilerParams(vmem_limit_bytes=16 << 20),
        name="first_frames",
    )(flag, halo, partial, coefficients, table, spectra)

    items = fft // (2 * devices)
    outgoing = spectra.reshape(devices, 2 * items, frames, inputs)
    received = lax.all_to_all(outgoing, ("tm", "input"), 0, 0, tiled=True)
    received = received.reshape(tm_count, input_count, items, 2, frames, inputs)
    depth = 2 * tm_count * frames
    width = input_count * inputs
    blocks = (width // BLOCK) ** 2
    return pl.pallas_call(
        correlate_kernel,
        in_specs=[vmem],
        out_specs=hbm,
        out_shape=jax.ShapeDtypeStruct((items, 2, width, width), jnp.bfloat16),
        scratch_shapes=[
            pltpu.VMEM((items, depth, width), jnp.bfloat16),
            pltpu.VMEM((items, width, depth), jnp.bfloat16),
            pltpu.VMEM((items, depth, width), jnp.bfloat16),
            pltpu.VMEM((items, 2, width, width), jnp.bfloat16),
            pltpu.SemaphoreType.DMA((2 * items * blocks,)),
        ],
        compiler_params=pltpu.CompilerParams(vmem_limit_bytes=36 << 20),
        name="correlate",
    )(received)


def solution(mesh):
    in_specs = (P("input", "tm"), P())
    out_specs = P(("tm", "input"), None, None, None)
    return jax.shard_map(local, mesh=mesh, in_specs=in_specs, out_specs=out_specs, check_vma=False)
```

```python
import functools

import jax
import jax.numpy as jnp
import ml_dtypes
import numpy as np
from jax import lax
from jax.experimental import pallas as pl
from jax.experimental.pallas import tpu as pltpu
from jax.sharding import PartitionSpec as P

GROUP = 8
BLOCK = 256
ROWS = 16
LANES = 128
AHEAD = 3


def dft_table(length):
    channel = np.arange(length) // 2
    phase = channel[:, None] * np.arange(length)[None, :] % length
    angles = phase * (2.0 * np.pi / length)
    real = (np.arange(length) % 2 == 0)[:, None]
    values = np.where(real, np.cos(angles), -np.sin(angles)) / np.sqrt(length)
    return (values.astype(ml_dtypes.bfloat16).astype(np.float32) / 8.0).astype(ml_dtypes.bfloat16)


def edge_frames(frames):
    return [*range(AHEAD, GROUP), *range(frames, frames + AHEAD)]


def tails_kernel(samples_ref, last_ref, first_ref, last, first, sems):
    count = samples_ref.shape[1]
    copies = [
        pltpu.make_async_copy(
            samples_ref.at[:, pl.ds(count - last.shape[1], last.shape[1])], last, sems.at[0]
        ),
        pltpu.make_async_copy(samples_ref.at[:, pl.ds(0, first.shape[1])], first, sems.at[1]),
    ]
    for copy in copies:
        copy.start()
    for copy, source, target in zip(copies, (last, first), (last_ref, first_ref), strict=True):
        copy.wait()
        target[...] = source[...].astype(jnp.float32).astype(jnp.bfloat16)


def transform(filt, table_ref, spread, stage, spectra_ref, group, sem):
    frames, inputs, fft = filt.shape
    for f in range(0, frames, 2):
        pair = filt[f : f + 2].reshape(2 * inputs, fft)
        spectra = lax.dot_general(
            table_ref[...], pair, (((1,), (1,)), ((), ())), preferred_element_type=jnp.float32
        )
        spread[pl.ds(f, fft, stride=frames), :] = spectra[:, :inputs]
        spread[pl.ds(f + 1, fft, stride=frames), :] = spectra[:, inputs:]
    block = spread[...].reshape(fft, frames, inputs).astype(jnp.bfloat16)
    stage[...] = block
    copy = pltpu.make_async_copy(
        stage, spectra_ref.at[:, pl.ds(group * frames, frames), :], sem
    )
    copy.start()
    return copy


def own_kernel(
    samples_ref, coef_hbm, table_hbm, spectra_ref, partial_ref,
    coef_ref, table_ref, held, filt, spread, stage, sems, out_sems,
):
    taps, fft = coef_ref.shape
    groups, inputs, span = held.shape
    frames = groups * GROUP
    edge = edge_frames(frames)
    coef_copy = pltpu.make_async_copy(coef_hbm, coef_ref, sems.at[groups])
    coef_copy.start()
    copies = []
    for g in range(groups):
        copy = pltpu.make_async_copy(
            samples_ref.at[:, pl.ds(g * span, span)], held.at[g], sems.at[g]
        )
        copy.start()
        copies.append(copy)
    table_copy = pltpu.make_async_copy(table_hbm, table_ref, sems.at[groups + 1])
    table_copy.start()
    coef_copy.wait()
    results = []

    copies[0].wait()
    for g in [*range(1, groups), 0]:
        if g:
            copies[g].wait()

        def rows_step(it, carry, g=g):
            rows = pl.ds(pl.multiple_of(it * ROWS, ROWS), ROWS)
            for n0 in range(0, fft, LANES):
                coefs = [coef_ref[p : p + 1, n0 : n0 + LANES] for p in range(taps)]

                def frame(f):
                    where, k = f // GROUP, f % GROUP
                    return held[where, rows, k * fft + n0 : k * fft + n0 + LANES].astype(jnp.float32)

                def share(f, known):
                    total = None
                    for p in range(taps):
                        if f - p in known:
                            term = coefs[p] * known[f - p]
                            total = term if total is None else total + term
                    return total

                if g == 0:
                    known = {f: frame(f) for f in range(GROUP)}
                    for slot, f in enumerate(edge[:-AHEAD]):
                        partial_ref[slot, rows, n0 : n0 + LANES] = share(f, known)
                    known = {f: frame(f) for f in range(frames + 1 - taps, frames)}
                    for slot, f in enumerate(edge[-AHEAD:]):
                        partial_ref[slot + GROUP - AHEAD, rows, n0 : n0 + LANES] = share(f, known)
                else:
                    known = {f: frame(f) for f in range(g * GROUP + 1 - taps, g * GROUP)}
                    for slot in range(GROUP):
                        f = g * GROUP + slot
                        known[f] = frame(f)
                        filt[slot, rows, n0 : n0 + LANES] = share(f, known).astype(jnp.bfloat16)
            return carry

        lax.fori_loop(0, inputs // ROWS, rows_step, 0)
        if g:
            if g == 1:
                table_copy.wait()
            results.append(
                transform(filt, table_ref, spread, stage.at[g - 1], spectra_ref, g, out_sems.at[g - 1])
            )
    for copy in results:
        copy.wait()


def edge_kernel(
    has_behind_ref, has_own_ref, behind_ref, ahead_ref, partial_ref, coef_ref, table_ref, _, spectra_ref,
    filt, spread, stage, sem, *, frames,
):
    taps, fft = coef_ref.shape
    inputs = behind_ref.shape[0]
    past = behind_ref.shape[1] // fft
    has_behind, has_own = has_behind_ref[0], has_own_ref[0]

    def rows_step(it, carry):
        rows = pl.ds(pl.multiple_of(it * ROWS, ROWS), ROWS)
        for n0 in range(0, fft, LANES):
            coefs = [coef_ref[p : p + 1, n0 : n0 + LANES] for p in range(taps)]
            masked = [coef * has_behind for coef in coefs]

            def frame(ref, k):
                return ref[rows, k * fft + n0 : k * fft + n0 + LANES].astype(jnp.float32)

            behind = [frame(behind_ref, k) for k in range(past)]
            ahead = [frame(ahead_ref, k) for k in range(AHEAD)]
            for slot, f in enumerate(edge_frames(frames)):
                total = partial_ref[slot, rows, n0 : n0 + LANES]
                if f < frames:
                    for p in range(f + 1, taps):
                        total = total + masked[p] * behind[f - p + past]
                else:
                    total = total * has_own
                    for p in range(f - frames + 1):
                        total = total + coefs[p] * ahead[f - frames - p]
                filt[slot, rows, n0 : n0 + LANES] = total.astype(jnp.bfloat16)
        return carry

    lax.fori_loop(0, inputs // ROWS, rows_step, 0)
    transform(filt, table_ref, spread, stage, spectra_ref, 0, sem).wait()


def correlate_kernel(recv_ref, out_ref, held, turned, swapped, stage, sems):
    tm_count, input_count, items, _, frames, inputs = recv_ref.shape
    half = tm_count * frames
    width = input_count * inputs
    scale = 1.0 / half
    copies = []

    def give(c, part, i, j, value):
        rows, cols = pl.ds(i, BLOCK), pl.ds(j, BLOCK)
        stage[c, part, rows, cols] = value.astype(jnp.bfloat16)
        copy = pltpu.make_async_copy(
            stage.at[c, part, rows, cols], out_ref.at[c, part, rows, cols], sems.at[len(copies)]
        )
        copy.start()
        copies.append(copy)

    for c in range(items):
        for r in range(2):
            for a in range(tm_count):
                for b in range(input_count):
                    rows = slice(r * half + a * frames, r * half + (a + 1) * frames)
                    cols = slice(b * inputs, (b + 1) * inputs)
                    held[c, rows, cols] = recv_ref[a, b, c, r]
        turned[c] = held[c].T
        swapped[c, :half] = -held[c, half:]
        swapped[c, half:] = held[c, :half]
        for i in range(0, width, BLOCK):
            for j in range(i, width, BLOCK):
                left = turned[c, i : i + BLOCK]
                real = scale * jnp.dot(
                    left, held[c, :, j : j + BLOCK], preferred_element_type=jnp.float32
                )
                imag = scale * jnp.dot(
                    left, swapped[c, :, j : j + BLOCK], preferred_element_type=jnp.float32
                )
                give(c, 0, i, j, real)
                give(c, 1, i, j, imag)
                if j > i:
                    give(c, 0, j, i, real.T)
                    give(c, 1, j, i, -imag.T)
    for copy in copies:
        copy.wait()


def local(samples, coefficients):
    inputs, sample_count = samples.shape
    taps, fft = coefficients.shape
    frames = sample_count // fft
    tm_count = lax.axis_size("tm")
    input_count = lax.axis_size("input")
    devices = tm_count * input_count
    groups = frames // GROUP
    past = (taps - 1 - AHEAD) * fft
    ahead = AHEAD * fft
    table = jnp.asarray(dft_table(fft))
    vmem = pl.BlockSpec(memory_space=pltpu.VMEM)
    smem = pl.BlockSpec(memory_space=pltpu.SMEM)
    hbm = pl.BlockSpec(memory_space=pltpu.HBM)

    ring = [(i, (i + 1) % tm_count) for i in range(tm_count)]
    own_tm = lax.axis_index("tm")
    has_behind = jnp.where(own_tm > 0, 1.0, 0.0).astype(jnp.float32).reshape(1)
    has_own = jnp.where(own_tm < tm_count - 1, 1.0, 0.0).astype(jnp.float32).reshape(1)
    spectra_type = pltpu.HBM((fft, frames, inputs), jnp.bfloat16)
    in_hbm = lambda array: pltpu.with_memory_space_constraint(array, pltpu.HBM)
    filt = pltpu.VMEM((GROUP, inputs, fft), jnp.bfloat16)
    spread = pltpu.VMEM((fft * GROUP, inputs), jnp.float32)
    last, first = pl.pallas_call(
        tails_kernel,
        in_specs=[hbm],
        out_specs=[vmem, vmem],
        out_shape=[
            pltpu.VMEM((inputs, past), jnp.bfloat16),
            pltpu.VMEM((inputs, ahead), jnp.bfloat16),
        ],
        scratch_shapes=[
            pltpu.VMEM((inputs, past), jnp.int32),
            pltpu.VMEM((inputs, ahead), jnp.int32),
            pltpu.SemaphoreType.DMA((2,)),
        ],
        compiler_params=pltpu.CompilerParams(vmem_limit_bytes=8 << 20),
        name="tails",
    )(in_hbm(samples))
    from_behind = lax.ppermute(last, "tm", ring)
    from_ahead = lax.ppermute(first, "tm", [(b, a) for a, b in ring])

    spectra, partial = pl.pallas_call(
        own_kernel,
        in_specs=[hbm, hbm, hbm],
        out_specs=[hbm, vmem],
        out_shape=[spectra_type, pltpu.VMEM((GROUP, inputs, fft), jnp.float32)],
        scratch_shapes=[
            pltpu.VMEM((taps, fft), jnp.float32),
            pltpu.VMEM((fft, fft), jnp.bfloat16),
            pltpu.VMEM((groups, inputs, GROUP * fft), jnp.int32),
            filt,
            spread,
            pltpu.VMEM((groups - 1, fft, GROUP, inputs), jnp.bfloat16),
            pltpu.SemaphoreType.DMA((groups + 2,)),
            pltpu.SemaphoreType.DMA((groups - 1,)),
        ],
        compiler_params=pltpu.CompilerParams(vmem_limit_bytes=24 << 20),
        name="own_frames",
    )(in_hbm(samples), in_hbm(coefficients), in_hbm(table))
    spectra = pl.pallas_call(
        functools.partial(edge_kernel, frames=frames),
        in_specs=[smem] * 2 + [vmem] * 5 + [hbm],
        out_specs=hbm,
        out_shape=spectra_type,
        scratch_shapes=[
            filt,
            spread,
            pltpu.VMEM((fft, GROUP, inputs), jnp.bfloat16),
            pltpu.SemaphoreType.DMA,
        ],
        input_output_aliases={7: 0},
        compiler_params=pltpu.CompilerParams(vmem_limit_bytes=16 << 20),
        name="edge_frames",
    )(has_behind, has_own, from_behind, from_ahead, partial, coefficients, table, spectra)

    items = fft // (2 * devices)
    outgoing = spectra.reshape(devices, 2 * items, frames, inputs)
    received = lax.all_to_all(outgoing, ("tm", "input"), 0, 0, tiled=True)
    received = received.reshape(tm_count, input_count, items, 2, frames, inputs)
    depth = 2 * tm_count * frames
    width = input_count * inputs
    blocks = (width // BLOCK) ** 2
    return pl.pallas_call(
        correlate_kernel,
        in_specs=[vmem],
        out_specs=hbm,
        out_shape=jax.ShapeDtypeStruct((items, 2, width, width), jnp.bfloat16),
        scratch_shapes=[
            pltpu.VMEM((items, depth, width), jnp.bfloat16),
            pltpu.VMEM((items, width, depth), jnp.bfloat16),
            pltpu.VMEM((items, depth, width), jnp.bfloat16),
            pltpu.VMEM((items, 2, width, width), jnp.bfloat16),
            pltpu.SemaphoreType.DMA((2 * items * blocks,)),
        ],
        compiler_params=pltpu.CompilerParams(vmem_limit_bytes=36 << 20),
        name="correlate",
    )(received)


def solution(mesh):
    in_specs = (P("input", "tm"), P())
    out_specs = P(("tm", "input"), None, None, None)
    return jax.shard_map(local, mesh=mesh, in_specs=in_specs, out_specs=out_specs, check_vma=False)
```

```python
import functools

import jax
import jax.numpy as jnp
import ml_dtypes
import numpy as np
from jax import lax
from jax.experimental import pallas as pl
from jax.experimental.pallas import tpu as pltpu
from jax.sharding import PartitionSpec as P

GROUP = 8
BLOCK = 256
ROWS = 16
LANES = 128
AHEAD = 3


def half_tables(length, items):
    assert items == 2
    channel = np.arange(length // 2).reshape(-1, items).T
    phase = channel[:, :, None] * np.arange(length // 2) % length
    angles = phase * (2.0 * np.pi / length)
    values = np.stack([np.cos(angles), -np.sin(angles)], axis=1) / np.sqrt(length)
    values = values.astype(ml_dtypes.bfloat16).astype(np.float32) / 8.0
    return values.reshape(items, -1, length // 2).astype(ml_dtypes.bfloat16)


def transform(filt, h, f, table_ref, spread):
    _, frames, inputs, half = filt.shape
    pair = filt[h, pl.ds(f, 2)].reshape(2 * inputs, half)
    spectra = lax.dot_general(
        table_ref[h], pair, (((1,), (1,)), ((), ())), preferred_element_type=jnp.float32
    )
    devices = half // 2
    stride = 4 * frames
    for r in range(2):
        rows = spectra[r * devices : (r + 1) * devices]
        first = (2 * h + r) * frames + f
        spread[pl.ds(first, devices, stride=stride), :] = rows[:, :inputs]
        spread[pl.ds(first + 1, devices, stride=stride), :] = rows[:, inputs:]


def pack(spread, stage, part, parts):
    rows, frames, inputs = stage.shape
    count = rows // parts
    block = spread[pl.ds(part * count * frames, count * frames), :]
    stage[pl.ds(part * count, count)] = block.reshape(count, frames, inputs).astype(jnp.bfloat16)


def halves(low, high):
    return (low + high).astype(jnp.bfloat16), (low - high).astype(jnp.bfloat16)


def edge_frames(frames):
    return [*range(AHEAD, GROUP), *range(frames, frames + AHEAD)]


def tails_kernel(samples_ref, last_ref, first_ref, last, first, sems):
    count = samples_ref.shape[1]
    copies = [
        pltpu.make_async_copy(
            samples_ref.at[:, pl.ds(count - last.shape[1], last.shape[1])], last, sems.at[0]
        ),
        pltpu.make_async_copy(samples_ref.at[:, pl.ds(0, first.shape[1])], first, sems.at[1]),
    ]
    for copy in copies:
        copy.start()
    for copy, source, target in zip(copies, (last, first), (last_ref, first_ref), strict=True):
        copy.wait()
        target[...] = source[...].astype(jnp.float32).astype(jnp.bfloat16)


def own_kernel(
    samples_ref, coef_hbm, table_hbm, spectra_ref, partial_ref,
    coef_ref, table_ref, held, filts, spreads, stage, sems, out_sems,
):
    taps, fft = coef_ref.shape
    groups, inputs, span = held.shape
    frames = groups * GROUP
    half = fft // 2
    edge = edge_frames(frames)
    steps = inputs // ROWS
    coef_copy = pltpu.make_async_copy(coef_hbm, coef_ref, sems.at[groups])
    coef_copy.start()
    copies = []
    for g in range(groups):
        copy = pltpu.make_async_copy(
            samples_ref.at[:, pl.ds(g * span, span)], held.at[g], sems.at[g]
        )
        copy.start()
        copies.append(copy)
    table_copy = pltpu.make_async_copy(table_hbm, table_ref, sems.at[groups + 1])
    table_copy.start()
    coef_copy.wait()

    def filter_rows(g, it):
        rows = pl.ds(pl.multiple_of(it * ROWS, ROWS), ROWS)

        def frame(f, n):
            where, k = f // GROUP, f % GROUP
            return held[where, rows, k * fft + n : k * fft + n + LANES].astype(jnp.float32)

        def share(f, known, n):
            total = None
            for p in range(taps):
                if f - p in known:
                    term = coef_ref[p : p + 1, n : n + LANES] * known[f - p]
                    total = term if total is None else total + term
            return total

        if g == 0:
            for n in range(0, fft, LANES):
                known = {f: frame(f, n) for f in range(GROUP)}
                for slot, f in enumerate(edge[:-AHEAD]):
                    partial_ref[slot, rows, n : n + LANES] = share(f, known, n)
                known = {f: frame(f, n) for f in range(frames + 1 - taps, frames)}
                for slot, f in enumerate(edge[-AHEAD:]):
                    partial_ref[slot + GROUP - AHEAD, rows, n : n + LANES] = share(f, known, n)
            return
        filt = filts[g % 2]
        for n in range(0, half, LANES):
            known = [
                {f: frame(f, n + m) for f in range(g * GROUP + 1 - taps, g * GROUP)} for m in (0, half)
            ]
            for slot in range(GROUP):
                f = g * GROUP + slot
                totals = []
                for m, seen in zip((0, half), known, strict=True):
                    seen[f] = frame(f, n + m)
                    totals.append(share(f, seen, n + m))
                even, odd = halves(*totals)
                filt[0, slot, rows, n : n + LANES] = even
                filt[1, slot, rows, n : n + LANES] = odd

    results = []

    def send(g):
        copy = pltpu.make_async_copy(
            stage.at[g - 1], spectra_ref.at[:, pl.ds(g * GROUP, GROUP), :], out_sems.at[g - 1]
        )
        copy.start()
        results.append(copy)

    copies[0].wait()
    order = [*range(1, groups), 0]
    for at, g in enumerate(order):
        if g:
            copies[g].wait()
        if at == 1:
            table_copy.wait()
        if at >= 3:
            send(order[at - 3])

        def step(it, carry, at=at, g=g):
            if at >= 1:
                last = order[at - 1]
                transform(filts[last % 2], it % 2, it // 2 * 2, table_ref, spreads[last % 2])
            if at >= 2:
                before = order[at - 2]
                pack(spreads[before % 2], stage.at[before - 1], it, steps)
            filter_rows(g, it)
            return carry

        lax.fori_loop(0, steps, step, 0)
    send(order[-3])
    pack(spreads[order[-2] % 2], stage.at[order[-2] - 1], 0, 1)
    send(order[-2])
    for copy in results:
        copy.wait()


def edge_kernel(
    has_behind_ref, has_own_ref, behind_ref, ahead_ref, partial_ref, coef_ref, table_ref, _, spectra_ref,
    filt, spread, stage, sems, *, frames,
):
    taps, fft = coef_ref.shape
    half = fft // 2
    inputs = behind_ref.shape[0]
    past = behind_ref.shape[1] // fft
    has_behind, has_own = has_behind_ref[0], has_own_ref[0]
    edge = edge_frames(frames)

    def total(slot, rows, n):
        f = edge[slot]
        value = partial_ref[slot, rows, n : n + LANES]
        if f < frames:
            for p in range(f + 1, taps):
                k = f - p + past
                sample = behind_ref[rows, k * fft + n : k * fft + n + LANES].astype(jnp.float32)
                value = value + (coef_ref[p : p + 1, n : n + LANES] * has_behind) * sample
        else:
            value = value * has_own
            for p in range(f - frames + 1):
                k = f - frames - p
                sample = ahead_ref[rows, k * fft + n : k * fft + n + LANES].astype(jnp.float32)
                value = value + coef_ref[p : p + 1, n : n + LANES] * sample
        return value

    for slot in range(0, GROUP, 2):
        for i in range(0, inputs, ROWS):
            rows = slice(i, i + ROWS)
            for n in range(0, half, LANES):
                for s in (slot, slot + 1):
                    even, odd = halves(total(s, rows, n), total(s, rows, n + half))
                    filt[0, s, rows, n : n + LANES] = even
                    filt[1, s, rows, n : n + LANES] = odd
        for h in range(2):
            transform(filt, h, slot, table_ref, spread)
    parts = sems.shape[0]
    copies = []
    for part in range(parts):
        pack(spread, stage, part, parts)
        rows = pl.ds(part * (fft // parts), fft // parts)
        copy = pltpu.make_async_copy(
            stage.at[rows], spectra_ref.at[rows, pl.ds(0, GROUP), :], sems.at[part]
        )
        copy.start()
        copies.append(copy)
    for copy in copies:
        copy.wait()


def correlate_kernel(recv_ref, out_ref, held, turned, swapped, stage, sems):
    tm_count, input_count, items, _, frames, inputs = recv_ref.shape
    half = tm_count * frames
    width = input_count * inputs
    scale = 1.0 / half
    copies = []

    def give(c, part, i, j, value):
        rows, cols = pl.ds(i, BLOCK), pl.ds(j, BLOCK)
        stage[c, part, rows, cols] = value.astype(jnp.bfloat16)
        copy = pltpu.make_async_copy(
            stage.at[c, part, rows, cols], out_ref.at[c, part, rows, cols], sems.at[len(copies)]
        )
        copy.start()
        copies.append(copy)

    for c in range(items):
        for r in range(2):
            for a in range(tm_count):
                for b in range(input_count):
                    rows = slice(r * half + a * frames, r * half + (a + 1) * frames)
                    cols = slice(b * inputs, (b + 1) * inputs)
                    held[c, rows, cols] = recv_ref[a, b, c, r]
        turned[c] = held[c].T
        swapped[c, :half] = -held[c, half:]
        swapped[c, half:] = held[c, :half]
        for i in range(0, width, BLOCK):
            for j in range(i, width, BLOCK):
                left = turned[c, i : i + BLOCK]
                real = scale * jnp.dot(
                    left, held[c, :, j : j + BLOCK], preferred_element_type=jnp.float32
                )
                imag = scale * jnp.dot(
                    left, swapped[c, :, j : j + BLOCK], preferred_element_type=jnp.float32
                )
                give(c, 0, i, j, real)
                give(c, 1, i, j, imag)
                if j > i:
                    give(c, 0, j, i, real.T)
                    give(c, 1, j, i, -imag.T)
    for copy in copies:
        copy.wait()


def local(samples, coefficients):
    inputs, sample_count = samples.shape
    taps, fft = coefficients.shape
    frames = sample_count // fft
    tm_count = lax.axis_size("tm")
    input_count = lax.axis_size("input")
    devices = tm_count * input_count
    groups = frames // GROUP
    past = (taps - 1 - AHEAD) * fft
    ahead = AHEAD * fft
    items = fft // (2 * devices)
    table = jnp.asarray(half_tables(fft, items))
    vmem = pl.BlockSpec(memory_space=pltpu.VMEM)
    smem = pl.BlockSpec(memory_space=pltpu.SMEM)
    hbm = pl.BlockSpec(memory_space=pltpu.HBM)

    ring = [(i, (i + 1) % tm_count) for i in range(tm_count)]
    own_tm = lax.axis_index("tm")
    has_behind = jnp.where(own_tm > 0, 1.0, 0.0).astype(jnp.float32).reshape(1)
    has_own = jnp.where(own_tm < tm_count - 1, 1.0, 0.0).astype(jnp.float32).reshape(1)
    spectra_type = pltpu.HBM((fft, frames, inputs), jnp.bfloat16)
    in_hbm = lambda array: pltpu.with_memory_space_constraint(array, pltpu.HBM)
    filt = pltpu.VMEM((2, GROUP, inputs, fft // 2), jnp.bfloat16)
    spread = pltpu.VMEM((fft * GROUP, inputs), jnp.float32)
    last, first = pl.pallas_call(
        tails_kernel,
        in_specs=[hbm],
        out_specs=[vmem, vmem],
        out_shape=[
            pltpu.VMEM((inputs, past), jnp.bfloat16),
            pltpu.VMEM((inputs, ahead), jnp.bfloat16),
        ],
        scratch_shapes=[
            pltpu.VMEM((inputs, past), jnp.int32),
            pltpu.VMEM((inputs, ahead), jnp.int32),
            pltpu.SemaphoreType.DMA((2,)),
        ],
        compiler_params=pltpu.CompilerParams(vmem_limit_bytes=8 << 20),
        name="tails",
    )(in_hbm(samples))
    from_behind = lax.ppermute(last, "tm", ring)
    from_ahead = lax.ppermute(first, "tm", [(b, a) for a, b in ring])

    spectra, partial = pl.pallas_call(
        own_kernel,
        in_specs=[hbm, hbm, hbm],
        out_specs=[hbm, vmem],
        out_shape=[spectra_type, pltpu.VMEM((GROUP, inputs, fft), jnp.float32)],
        scratch_shapes=[
            pltpu.VMEM((taps, fft), jnp.float32),
            pltpu.VMEM(table.shape, jnp.bfloat16),
            pltpu.VMEM((groups, inputs, GROUP * fft), jnp.int32),
            [filt, filt],
            [spread, spread],
            pltpu.VMEM((groups - 1, fft, GROUP, inputs), jnp.bfloat16),
            pltpu.SemaphoreType.DMA((groups + 2,)),
            pltpu.SemaphoreType.DMA((groups - 1,)),
        ],
        compiler_params=pltpu.CompilerParams(vmem_limit_bytes=24 << 20),
        name="own_frames",
    )(in_hbm(samples), in_hbm(coefficients), in_hbm(table))
    spectra = pl.pallas_call(
        functools.partial(edge_kernel, frames=frames),
        in_specs=[smem] * 2 + [vmem] * 5 + [hbm],
        out_specs=hbm,
        out_shape=spectra_type,
        scratch_shapes=[
            filt,
            spread,
            pltpu.VMEM((fft, GROUP, inputs), jnp.bfloat16),
            pltpu.SemaphoreType.DMA((4,)),
        ],
        input_output_aliases={7: 0},
        compiler_params=pltpu.CompilerParams(vmem_limit_bytes=16 << 20),
        name="edge_frames",
    )(has_behind, has_own, from_behind, from_ahead, partial, coefficients, table, spectra)

    outgoing = spectra.reshape(devices, 2 * items, frames, inputs)
    received = lax.all_to_all(outgoing, ("tm", "input"), 0, 0, tiled=True)
    received = received.reshape(tm_count, input_count, items, 2, frames, inputs)
    depth = 2 * tm_count * frames
    width = input_count * inputs
    blocks = (width // BLOCK) ** 2
    return pl.pallas_call(
        correlate_kernel,
        in_specs=[vmem],
        out_specs=hbm,
        out_shape=jax.ShapeDtypeStruct((items, 2, width, width), jnp.bfloat16),
        scratch_shapes=[
            pltpu.VMEM((items, depth, width), jnp.bfloat16),
            pltpu.VMEM((items, width, depth), jnp.bfloat16),
            pltpu.VMEM((items, depth, width), jnp.bfloat16),
            pltpu.VMEM((items, 2, width, width), jnp.bfloat16),
            pltpu.SemaphoreType.DMA((2 * items * blocks,)),
        ],
        compiler_params=pltpu.CompilerParams(vmem_limit_bytes=36 << 20),
        name="correlate",
    )(received)


def solution(mesh):
    in_specs = (P("input", "tm"), P())
    out_specs = P(("tm", "input"), None, None, None)
    return jax.shard_map(local, mesh=mesh, in_specs=in_specs, out_specs=out_specs, check_vma=False)
```

```python
import functools

import jax
import jax.numpy as jnp
import ml_dtypes
import numpy as np
from jax import lax
from jax.experimental import pallas as pl
from jax.experimental.pallas import tpu as pltpu
from jax.sharding import PartitionSpec as P

GROUP = 8
BLOCK = 256
ROWS = 16
LANES = 128
AHEAD = 3


def dft_table(length):
    channel = np.arange(length) // 2
    phase = channel[:, None] * np.arange(length)[None, :] % length
    angles = phase * (2.0 * np.pi / length)
    real = (np.arange(length) % 2 == 0)[:, None]
    values = np.where(real, np.cos(angles), -np.sin(angles)) / np.sqrt(length)
    return (values.astype(ml_dtypes.bfloat16).astype(np.float32) / 8.0).astype(ml_dtypes.bfloat16)


def edge_frames(frames):
    return [*range(AHEAD, GROUP), *range(frames, frames + AHEAD)]


def tails_kernel(samples_ref, last_ref, first_ref, last, first, sems):
    count = samples_ref.shape[1]
    copies = [
        pltpu.make_async_copy(
            samples_ref.at[:, pl.ds(count - last.shape[1], last.shape[1])], last, sems.at[0]
        ),
        pltpu.make_async_copy(samples_ref.at[:, pl.ds(0, first.shape[1])], first, sems.at[1]),
    ]
    for copy in copies:
        copy.start()
    for copy, source, target in zip(copies, (last, first), (last_ref, first_ref), strict=True):
        copy.wait()
        target[...] = source[...].astype(jnp.float32).astype(jnp.bfloat16)


def transform_pair(filt, f, table_ref, spread):
    frames, inputs, fft = filt.shape
    pair = filt[f : f + 2].reshape(2 * inputs, fft)
    spectra = lax.dot_general(
        table_ref[...], pair, (((1,), (1,)), ((), ())), preferred_element_type=jnp.float32
    )
    spread[pl.ds(f, fft, stride=frames), :] = spectra[:, :inputs]
    spread[pl.ds(f + 1, fft, stride=frames), :] = spectra[:, inputs:]


def pack(spread, stage, part, parts):
    rows, frames, inputs = stage.shape
    count = rows // parts
    block = spread[part * count * frames : (part + 1) * count * frames, :]
    stage[part * count : (part + 1) * count] = block.reshape(count, frames, inputs).astype(
        jnp.bfloat16
    )


def own_kernel(
    samples_ref, coef_hbm, table_hbm, spectra_ref, partial_ref,
    coef_ref, table_ref, held, filts, spreads, stage, sems, out_sems,
):
    taps, fft = coef_ref.shape
    groups, inputs, span = held.shape
    frames = groups * GROUP
    edge = edge_frames(frames)

    def load(g):
        copy = pltpu.make_async_copy(
            samples_ref.at[:, pl.ds(g * span, span)], held.at[g], sems.at[g]
        )
        copy.start()
        return copy

    coef_copy = pltpu.make_async_copy(coef_hbm, coef_ref, sems.at[groups])
    coef_copy.start()
    loads = [load(0), load(1)]
    table_copy = pltpu.make_async_copy(table_hbm, table_ref, sems.at[groups + 1])
    table_copy.start()

    def filter_rows(g, i):
        rows = slice(i, i + ROWS)
        for n in range(0, fft, LANES):
            coefs = [coef_ref[p : p + 1, n : n + LANES] for p in range(taps)]

            def frame(f):
                where, k = f // GROUP, f % GROUP
                return held[where, rows, k * fft + n : k * fft + n + LANES].astype(jnp.float32)

            def share(f, known):
                total = None
                for p in range(taps):
                    if f - p in known:
                        term = coefs[p] * known[f - p]
                        total = term if total is None else total + term
                return total

            if g == 0:
                known = {f: frame(f) for f in range(GROUP)}
                for slot, f in enumerate(edge[:-AHEAD]):
                    partial_ref[slot, rows, n : n + LANES] = share(f, known)
                known = {f: frame(f) for f in range(frames + 1 - taps, frames)}
                for slot, f in enumerate(edge[-AHEAD:]):
                    partial_ref[slot + GROUP - AHEAD, rows, n : n + LANES] = share(f, known)
            else:
                known = {f: frame(f) for f in range(g * GROUP + 1 - taps, g * GROUP)}
                for slot in range(GROUP):
                    f = g * GROUP + slot
                    known[f] = frame(f)
                    filts[g % 2][slot, rows, n : n + LANES] = share(f, known).astype(jnp.bfloat16)

    results = []

    def send(g):
        copy = pltpu.make_async_copy(
            stage.at[g - 1], spectra_ref.at[:, pl.ds(g * GROUP, GROUP), :], out_sems.at[g - 1]
        )
        copy.start()
        results.append(copy)

    coef_copy.wait()
    loads[0].wait()
    order = [*range(1, groups), 0]
    pairs = GROUP // 2
    share_rows = inputs // pairs
    for at, g in enumerate(order):
        if g:
            loads[g].wait()
            if g + 1 < groups:
                loads.append(load(g + 1))
        if at == 1:
            table_copy.wait()
        for pair in range(pairs):
            if at >= 1:
                last = order[at - 1]
                transform_pair(filts[last % 2], 2 * pair, table_ref, spreads[last % 2])
            if at >= 2:
                before = order[at - 2]
                pack(spreads[before % 2], stage.at[before - 1], pair, pairs)
            for i in range(pair * share_rows, (pair + 1) * share_rows, ROWS):
                filter_rows(g, i)
        if at >= 2:
            send(order[at - 2])
    pack(spreads[order[-2] % 2], stage.at[order[-2] - 1], 0, 1)
    send(order[-2])
    for copy in results:
        copy.wait()


def edge_kernel(
    has_behind_ref, has_own_ref, behind_ref, ahead_ref, partial_ref, coef_ref, table_ref, _, spectra_ref,
    masked_ref, filt, spread, stage, sems, *, frames,
):
    taps, fft = coef_ref.shape
    inputs = behind_ref.shape[0]
    past = behind_ref.shape[1] // fft
    has_own = has_own_ref[0]
    edge = edge_frames(frames)
    masked_ref[...] = coef_ref[...] * has_behind_ref[0]

    for slot in range(0, GROUP, 2):
        for i in range(0, inputs, ROWS):
            rows = slice(i, i + ROWS)
            for n in range(0, fft, LANES):
                lanes = slice(n, n + LANES)
                samples = {}

                def frame(f):
                    if f not in samples:
                        ref, k = (behind_ref, f + past) if f < 0 else (ahead_ref, f - frames)
                        value = ref[rows, k * fft + n : k * fft + n + LANES]
                        samples[f] = value.astype(jnp.float32)
                    return samples[f]

                for s in (slot, slot + 1):
                    f = edge[s]
                    value = partial_ref[s, rows, lanes]
                    if f < frames:
                        for p in range(f + 1, taps):
                            value = value + masked_ref[p : p + 1, lanes] * frame(f - p)
                    else:
                        value = value * has_own
                        for p in range(f - frames + 1):
                            value = value + coef_ref[p : p + 1, lanes] * frame(f - p)
                    filt[s, rows, lanes] = value.astype(jnp.bfloat16)
        transform_pair(filt, slot, table_ref, spread)
    parts = sems.shape[0]
    copies = []
    for part in range(parts):
        pack(spread, stage, part, parts)
        rows = pl.ds(part * (fft // parts), fft // parts)
        copy = pltpu.make_async_copy(
            stage.at[rows], spectra_ref.at[rows, pl.ds(0, GROUP), :], sems.at[part]
        )
        copy.start()
        copies.append(copy)
    for copy in copies:
        copy.wait()


def correlate_kernel(recv_ref, out_ref, held, turned, swapped, stage, sems):
    tm_count, input_count, items, _, frames, inputs = recv_ref.shape
    half = tm_count * frames
    width = input_count * inputs
    scale = 1.0 / half
    copies = []

    def give(c, part, i, j, value):
        rows, cols = pl.ds(i, BLOCK), pl.ds(j, BLOCK)
        stage[c, part, rows, cols] = value.astype(jnp.bfloat16)
        copy = pltpu.make_async_copy(
            stage.at[c, part, rows, cols], out_ref.at[c, part, rows, cols], sems.at[len(copies)]
        )
        copy.start()
        copies.append(copy)

    for c in range(items):
        for r in range(2):
            for a in range(tm_count):
                for b in range(input_count):
                    rows = slice(r * half + a * frames, r * half + (a + 1) * frames)
                    cols = slice(b * inputs, (b + 1) * inputs)
                    held[c, rows, cols] = recv_ref[a, b, c, r]
        turned[c] = held[c].T
        swapped[c, :half] = -held[c, half:]
        swapped[c, half:] = held[c, :half]
        for i in range(0, width, BLOCK):
            for j in range(i, width, BLOCK):
                left = turned[c, i : i + BLOCK]
                real = scale * jnp.dot(
                    left, held[c, :, j : j + BLOCK], preferred_element_type=jnp.float32
                )
                if j > i:
                    imag = scale * jnp.dot(
                        left, swapped[c, :, j : j + BLOCK], preferred_element_type=jnp.float32
                    )
                else:
                    cross = scale * jnp.dot(
                        turned[c, i : i + BLOCK, half:],
                        held[c, :half, j : j + BLOCK],
                        preferred_element_type=jnp.float32,
                    )
                    imag = cross - cross.T
                give(c, 0, i, j, real)
                give(c, 1, i, j, imag)
                if j > i:
                    give(c, 0, j, i, real.T)
                    give(c, 1, j, i, -imag.T)
    for copy in copies:
        copy.wait()


def local(samples, coefficients):
    inputs, sample_count = samples.shape
    taps, fft = coefficients.shape
    frames = sample_count // fft
    tm_count = lax.axis_size("tm")
    input_count = lax.axis_size("input")
    devices = tm_count * input_count
    groups = frames // GROUP
    past = (taps - 1 - AHEAD) * fft
    ahead = AHEAD * fft
    table = jnp.asarray(dft_table(fft))
    vmem = pl.BlockSpec(memory_space=pltpu.VMEM)
    smem = pl.BlockSpec(memory_space=pltpu.SMEM)
    hbm = pl.BlockSpec(memory_space=pltpu.HBM)

    ring = [(i, (i + 1) % tm_count) for i in range(tm_count)]
    own_tm = lax.axis_index("tm")
    has_behind = jnp.where(own_tm > 0, 1.0, 0.0).astype(jnp.float32).reshape(1)
    has_own = jnp.where(own_tm < tm_count - 1, 1.0, 0.0).astype(jnp.float32).reshape(1)
    spectra_type = pltpu.HBM((fft, frames, inputs), jnp.bfloat16)
    in_hbm = lambda array: pltpu.with_memory_space_constraint(array, pltpu.HBM)
    filt = pltpu.VMEM((GROUP, inputs, fft), jnp.bfloat16)
    spread = pltpu.VMEM((fft * GROUP, inputs), jnp.float32)
    last, first = pl.pallas_call(
        tails_kernel,
        in_specs=[hbm],
        out_specs=[vmem, vmem],
        out_shape=[
            pltpu.VMEM((inputs, past), jnp.bfloat16),
            pltpu.VMEM((inputs, ahead), jnp.bfloat16),
        ],
        scratch_shapes=[
            pltpu.VMEM((inputs, past), jnp.int32),
            pltpu.VMEM((inputs, ahead), jnp.int32),
            pltpu.SemaphoreType.DMA((2,)),
        ],
        compiler_params=pltpu.CompilerParams(vmem_limit_bytes=8 << 20),
        name="tails",
    )(in_hbm(samples))
    from_behind = lax.ppermute(last, "tm", ring)
    from_ahead = lax.ppermute(first, "tm", [(b, a) for a, b in ring])

    spectra, partial = pl.pallas_call(
        own_kernel,
        in_specs=[hbm, hbm, hbm],
        out_specs=[hbm, vmem],
        out_shape=[spectra_type, pltpu.VMEM((GROUP, inputs, fft), jnp.float32)],
        scratch_shapes=[
            pltpu.VMEM((taps, fft), jnp.float32),
            pltpu.VMEM((fft, fft), jnp.bfloat16),
            pltpu.VMEM((groups, inputs, GROUP * fft), jnp.int32),
            [filt, filt],
            [spread, spread],
            pltpu.VMEM((groups - 1, fft, GROUP, inputs), jnp.bfloat16),
            pltpu.SemaphoreType.DMA((groups + 2,)),
            pltpu.SemaphoreType.DMA((groups - 1,)),
        ],
        compiler_params=pltpu.CompilerParams(vmem_limit_bytes=24 << 20),
        name="own_frames",
    )(in_hbm(samples), in_hbm(coefficients), in_hbm(table))
    spectra = pl.pallas_call(
        functools.partial(edge_kernel, frames=frames),
        in_specs=[smem] * 2 + [vmem] * 5 + [hbm],
        out_specs=hbm,
        out_shape=spectra_type,
        scratch_shapes=[
            pltpu.VMEM((taps, fft), jnp.float32),
            filt,
            spread,
            pltpu.VMEM((fft, GROUP, inputs), jnp.bfloat16),
            pltpu.SemaphoreType.DMA((4,)),
        ],
        input_output_aliases={7: 0},
        compiler_params=pltpu.CompilerParams(vmem_limit_bytes=16 << 20),
        name="edge_frames",
    )(has_behind, has_own, from_behind, from_ahead, partial, coefficients, table, spectra)

    items = fft // (2 * devices)
    outgoing = spectra.reshape(devices, 2 * items, frames, inputs)
    received = lax.all_to_all(outgoing, ("tm", "input"), 0, 0, tiled=True)
    received = received.reshape(tm_count, input_count, items, 2, frames, inputs)
    depth = 2 * tm_count * frames
    width = input_count * inputs
    blocks = (width // BLOCK) ** 2
    return pl.pallas_call(
        correlate_kernel,
        in_specs=[vmem],
        out_specs=hbm,
        out_shape=jax.ShapeDtypeStruct((items, 2, width, width), jnp.bfloat16),
        scratch_shapes=[
            pltpu.VMEM((items, depth, width), jnp.bfloat16),
            pltpu.VMEM((items, width, depth), jnp.bfloat16),
            pltpu.VMEM((items, depth, width), jnp.bfloat16),
            pltpu.VMEM((items, 2, width, width), jnp.bfloat16),
            pltpu.SemaphoreType.DMA((2 * items * blocks,)),
        ],
        compiler_params=pltpu.CompilerParams(vmem_limit_bytes=36 << 20),
        name="correlate",
    )(received)


def solution(mesh):
    in_specs = (P("input", "tm"), P())
    out_specs = P(("tm", "input"), None, None, None)
    return jax.shard_map(local, mesh=mesh, in_specs=in_specs, out_specs=out_specs, check_vma=False)
```

```python
import functools

import jax
import jax.numpy as jnp
import ml_dtypes
import numpy as np
from jax import lax
from jax.experimental import pallas as pl
from jax.experimental.pallas import tpu as pltpu
from jax.sharding import PartitionSpec as P

GROUP = 8
BLOCK = 256
ROWS = 16
LANES = 128
AHEAD = 3


def dft_table(length):
    channel = np.arange(length) // 2
    phase = channel[:, None] * np.arange(length)[None, :] % length
    angles = phase * (2.0 * np.pi / length)
    real = (np.arange(length) % 2 == 0)[:, None]
    values = np.where(real, np.cos(angles), -np.sin(angles)) / np.sqrt(length)
    return (values.astype(ml_dtypes.bfloat16).astype(np.float32) / 8.0).astype(ml_dtypes.bfloat16)


def edge_frames(frames):
    return [*range(AHEAD, GROUP), *range(frames, frames + AHEAD)]


def tails_kernel(samples_ref, last_ref, first_ref, last, first, sems):
    count = samples_ref.shape[1]
    copies = [
        pltpu.make_async_copy(
            samples_ref.at[:, pl.ds(count - last.shape[1], last.shape[1])], last, sems.at[0]
        ),
        pltpu.make_async_copy(samples_ref.at[:, pl.ds(0, first.shape[1])], first, sems.at[1]),
    ]
    for copy in copies:
        copy.start()
    for copy, source, target in zip(copies, (last, first), (last_ref, first_ref), strict=True):
        copy.wait()
        target[...] = source[...].astype(jnp.float32).astype(jnp.bfloat16)


def transform_pair(filt, f, table_ref, spread):
    frames, inputs, fft = filt.shape
    pair = filt[f : f + 2].reshape(2 * inputs, fft)
    spectra = lax.dot_general(
        table_ref[...], pair, (((1,), (1,)), ((), ())), preferred_element_type=jnp.float32
    )
    spread[pl.ds(f, fft, stride=frames), :] = spectra[:, :inputs]
    spread[pl.ds(f + 1, fft, stride=frames), :] = spectra[:, inputs:]


def pack(spread, stage, part, parts):
    rows, frames, inputs = stage.shape
    count = rows // parts
    block = spread[part * count * frames : (part + 1) * count * frames, :]
    stage[part * count : (part + 1) * count] = block.reshape(count, frames, inputs).astype(
        jnp.bfloat16
    )


def own_kernel(
    samples_ref, coef_hbm, table_hbm, spectra_ref, partial_ref,
    coef_ref, table_ref, held, filts, spreads, stage, sems, out_sems,
):
    taps, fft = coef_ref.shape
    inputs, count = held.shape
    frames = count // fft
    groups = frames // GROUP
    span = GROUP * fft
    edge = edge_frames(frames)
    pairs = GROUP // 2
    chunk = inputs // pairs

    boxes = [(slice(k * chunk, (k + 1) * chunk), slice(0, 2 * span)) for k in range(pairs)]
    boxes += [(slice(0, inputs), slice(g * span, (g + 1) * span)) for g in range(2, groups)]
    loads = [
        pltpu.make_async_copy(
            samples_ref.at[pl.ds(r.start, r.stop - r.start), pl.ds(c.start, c.stop - c.start)],
            held.at[pl.ds(r.start, r.stop - r.start), pl.ds(c.start, c.stop - c.start)],
            sems.at[k],
        )
        for k, (r, c) in enumerate(boxes)
    ]
    coef_copy = pltpu.make_async_copy(coef_hbm, coef_ref, sems.at[len(loads)])
    table_copy = pltpu.make_async_copy(table_hbm, table_ref, sems.at[len(loads) + 1])
    coef_copy.start()
    loads[0].start()
    loads[1].start()
    table_copy.start()

    def arrive(k):
        loads[k].wait()
        if k + 2 < len(loads):
            loads[k + 2].start()

    def filter_rows(g, i):
        rows = slice(i, i + ROWS)
        for n in range(0, fft, LANES):
            coefs = [coef_ref[p : p + 1, n : n + LANES] for p in range(taps)]

            def frame(f):
                return held[rows, f * fft + n : f * fft + n + LANES].astype(jnp.float32)

            def share(f, known):
                total = None
                for p in range(taps):
                    if f - p in known:
                        term = coefs[p] * known[f - p]
                        total = term if total is None else total + term
                return total

            if g == 0:
                known = {f: frame(f) for f in range(GROUP)}
                for slot, f in enumerate(edge[:-AHEAD]):
                    partial_ref[slot, rows, n : n + LANES] = share(f, known)
                known = {f: frame(f) for f in range(frames + 1 - taps, frames)}
                for slot, f in enumerate(edge[-AHEAD:]):
                    partial_ref[slot + GROUP - AHEAD, rows, n : n + LANES] = share(f, known)
            else:
                known = {f: frame(f) for f in range(g * GROUP + 1 - taps, g * GROUP)}
                for slot in range(GROUP):
                    f = g * GROUP + slot
                    known[f] = frame(f)
                    filts[g % 2][slot, rows, n : n + LANES] = share(f, known).astype(jnp.bfloat16)

    results = []

    def send(g, part=0, parts=1):
        rows = pl.ds(part * (fft // parts), fft // parts)
        copy = pltpu.make_async_copy(
            stage.at[g - 1, rows],
            spectra_ref.at[rows, pl.ds(g * GROUP, GROUP), :],
            out_sems.at[len(results)],
        )
        copy.start()
        results.append(copy)

    coef_copy.wait()
    for g in range(1, groups):
        if g == 2:
            table_copy.wait()
        if g >= 2:
            arrive(pairs + g - 2)
        for pair in range(pairs):
            if g >= 2:
                transform_pair(filts[(g - 1) % 2], 2 * pair, table_ref, spreads[(g - 1) % 2])
            if g >= 3:
                pack(spreads[g % 2], stage.at[g - 3], pair, pairs)
            if g == 1:
                arrive(pair)
            for i in range(pair * chunk, (pair + 1) * chunk, ROWS):
                filter_rows(g, i)
        if g >= 3:
            send(g - 2)
    last = groups - 1
    step = chunk // 2
    for pair in range(pairs):
        transform_pair(filts[last % 2], 2 * pair, table_ref, spreads[last % 2])
        pack(spreads[(last - 1) % 2], stage.at[last - 2], pair, pairs)
        filter_rows(0, pair * step)
    send(last - 1)
    for pair in range(pairs):
        pack(spreads[last % 2], stage.at[last - 1], pair, pairs)
        send(last, pair, pairs)
        filter_rows(0, (pairs + pair) * step)
    for copy in results:
        copy.wait()


def edge_kernel(
    has_behind_ref, has_own_ref, behind_ref, ahead_ref, partial_ref, coef_ref, table_ref, _, spectra_ref,
    masked_ref, filt, spread, stage, sems, *, frames,
):
    taps, fft = coef_ref.shape
    inputs = behind_ref.shape[0]
    past = behind_ref.shape[1] // fft
    has_own = has_own_ref[0]
    edge = edge_frames(frames)
    masked_ref[...] = coef_ref[...] * has_behind_ref[0]

    for slot in range(0, GROUP, 2):
        for i in range(0, inputs, ROWS):
            rows = slice(i, i + ROWS)
            for n in range(0, fft, LANES):
                lanes = slice(n, n + LANES)
                samples = {}

                def frame(f):
                    if f not in samples:
                        ref, k = (behind_ref, f + past) if f < 0 else (ahead_ref, f - frames)
                        value = ref[rows, k * fft + n : k * fft + n + LANES]
                        samples[f] = value.astype(jnp.float32)
                    return samples[f]

                for s in (slot, slot + 1):
                    f = edge[s]
                    value = partial_ref[s, rows, lanes]
                    if f < frames:
                        for p in range(f + 1, taps):
                            value = value + masked_ref[p : p + 1, lanes] * frame(f - p)
                    else:
                        value = value * has_own
                        for p in range(f - frames + 1):
                            value = value + coef_ref[p : p + 1, lanes] * frame(f - p)
                    filt[s, rows, lanes] = value.astype(jnp.bfloat16)
        transform_pair(filt, slot, table_ref, spread)
    parts = sems.shape[0]
    copies = []
    for part in range(parts):
        pack(spread, stage, part, parts)
        rows = pl.ds(part * (fft // parts), fft // parts)
        copy = pltpu.make_async_copy(
            stage.at[rows], spectra_ref.at[rows, pl.ds(0, GROUP), :], sems.at[part]
        )
        copy.start()
        copies.append(copy)
    for copy in copies:
        copy.wait()


def correlate_kernel(recv_ref, out_ref, held, turned, swapped, stage, sems):
    tm_count, input_count, items, _, frames, inputs = recv_ref.shape
    half = tm_count * frames
    width = input_count * inputs
    scale = 1.0 / half
    copies = []

    def give(c, part, i, j, value):
        rows, cols = pl.ds(i, BLOCK), pl.ds(j, BLOCK)
        stage[c, part, rows, cols] = value.astype(jnp.bfloat16)
        copy = pltpu.make_async_copy(
            stage.at[c, part, rows, cols], out_ref.at[c, part, rows, cols], sems.at[len(copies)]
        )
        copy.start()
        copies.append(copy)

    for c in range(items):
        for r in range(2):
            for a in range(tm_count):
                for b in range(input_count):
                    rows = slice(r * half + a * frames, r * half + (a + 1) * frames)
                    cols = slice(b * inputs, (b + 1) * inputs)
                    held[c, rows, cols] = recv_ref[a, b, c, r]
        turned[c] = held[c].T
        swapped[c, :half] = -held[c, half:]
        swapped[c, half:] = held[c, :half]
        for i in range(0, width, BLOCK):
            for j in range(i, width, BLOCK):
                left = turned[c, i : i + BLOCK]
                real = scale * jnp.dot(
                    left, held[c, :, j : j + BLOCK], preferred_element_type=jnp.float32
                )
                if j > i:
                    imag = scale * jnp.dot(
                        left, swapped[c, :, j : j + BLOCK], preferred_element_type=jnp.float32
                    )
                else:
                    cross = scale * jnp.dot(
                        turned[c, i : i + BLOCK, half:],
                        held[c, :half, j : j + BLOCK],
                        preferred_element_type=jnp.float32,
                    )
                    imag = cross - cross.T
                give(c, 0, i, j, real)
                give(c, 1, i, j, imag)
                if j > i:
                    give(c, 0, j, i, real.T)
                    give(c, 1, j, i, -imag.T)
    for copy in copies:
        copy.wait()


def local(samples, coefficients):
    inputs, sample_count = samples.shape
    taps, fft = coefficients.shape
    frames = sample_count // fft
    tm_count = lax.axis_size("tm")
    input_count = lax.axis_size("input")
    devices = tm_count * input_count
    groups = frames // GROUP
    past = (taps - 1 - AHEAD) * fft
    ahead = AHEAD * fft
    table = jnp.asarray(dft_table(fft))
    vmem = pl.BlockSpec(memory_space=pltpu.VMEM)
    smem = pl.BlockSpec(memory_space=pltpu.SMEM)
    hbm = pl.BlockSpec(memory_space=pltpu.HBM)

    ring = [(i, (i + 1) % tm_count) for i in range(tm_count)]
    own_tm = lax.axis_index("tm")
    has_behind = jnp.where(own_tm > 0, 1.0, 0.0).astype(jnp.float32).reshape(1)
    has_own = jnp.where(own_tm < tm_count - 1, 1.0, 0.0).astype(jnp.float32).reshape(1)
    spectra_type = pltpu.HBM((fft, frames, inputs), jnp.bfloat16)
    in_hbm = lambda array: pltpu.with_memory_space_constraint(array, pltpu.HBM)
    filt = pltpu.VMEM((GROUP, inputs, fft), jnp.bfloat16)
    spread = pltpu.VMEM((fft * GROUP, inputs), jnp.float32)
    last, first = pl.pallas_call(
        tails_kernel,
        in_specs=[hbm],
        out_specs=[vmem, vmem],
        out_shape=[
            pltpu.VMEM((inputs, past), jnp.bfloat16),
            pltpu.VMEM((inputs, ahead), jnp.bfloat16),
        ],
        scratch_shapes=[
            pltpu.VMEM((inputs, past), jnp.int32),
            pltpu.VMEM((inputs, ahead), jnp.int32),
            pltpu.SemaphoreType.DMA((2,)),
        ],
        compiler_params=pltpu.CompilerParams(vmem_limit_bytes=8 << 20),
        name="tails",
    )(in_hbm(samples))
    from_behind = lax.ppermute(last, "tm", ring)
    from_ahead = lax.ppermute(first, "tm", [(b, a) for a, b in ring])

    spectra, partial = pl.pallas_call(
        own_kernel,
        in_specs=[hbm, hbm, hbm],
        out_specs=[hbm, vmem],
        out_shape=[spectra_type, pltpu.VMEM((GROUP, inputs, fft), jnp.float32)],
        scratch_shapes=[
            pltpu.VMEM((taps, fft), jnp.float32),
            pltpu.VMEM((fft, fft), jnp.bfloat16),
            pltpu.VMEM((inputs, sample_count), jnp.int32),
            [filt, filt],
            [spread, spread],
            pltpu.VMEM((groups - 1, fft, GROUP, inputs), jnp.bfloat16),
            pltpu.SemaphoreType.DMA((GROUP // 2 + groups,)),
            pltpu.SemaphoreType.DMA((groups + GROUP // 2,)),
        ],
        compiler_params=pltpu.CompilerParams(vmem_limit_bytes=24 << 20),
        name="own_frames",
    )(in_hbm(samples), in_hbm(coefficients), in_hbm(table))
    spectra = pl.pallas_call(
        functools.partial(edge_kernel, frames=frames),
        in_specs=[smem] * 2 + [vmem] * 5 + [hbm],
        out_specs=hbm,
        out_shape=spectra_type,
        scratch_shapes=[
            pltpu.VMEM((taps, fft), jnp.float32),
            filt,
            spread,
            pltpu.VMEM((fft, GROUP, inputs), jnp.bfloat16),
            pltpu.SemaphoreType.DMA((4,)),
        ],
        input_output_aliases={7: 0},
        compiler_params=pltpu.CompilerParams(vmem_limit_bytes=16 << 20),
        name="edge_frames",
    )(has_behind, has_own, from_behind, from_ahead, partial, coefficients, table, spectra)

    items = fft // (2 * devices)
    outgoing = spectra.reshape(devices, 2 * items, frames, inputs)
    received = lax.all_to_all(outgoing, ("tm", "input"), 0, 0, tiled=True)
    received = received.reshape(tm_count, input_count, items, 2, frames, inputs)
    depth = 2 * tm_count * frames
    width = input_count * inputs
    blocks = (width // BLOCK) ** 2
    return pl.pallas_call(
        correlate_kernel,
        in_specs=[vmem],
        out_specs=hbm,
        out_shape=jax.ShapeDtypeStruct((items, 2, width, width), jnp.bfloat16),
        scratch_shapes=[
            pltpu.VMEM((items, depth, width), jnp.bfloat16),
            pltpu.VMEM((items, width, depth), jnp.bfloat16),
            pltpu.VMEM((items, depth, width), jnp.bfloat16),
            pltpu.VMEM((items, 2, width, width), jnp.bfloat16),
            pltpu.SemaphoreType.DMA((2 * items * blocks,)),
        ],
        compiler_params=pltpu.CompilerParams(vmem_limit_bytes=36 << 20),
        name="correlate",
    )(received)


def solution(mesh):
    in_specs = (P("input", "tm"), P())
    out_specs = P(("tm", "input"), None, None, None)
    return jax.shard_map(local, mesh=mesh, in_specs=in_specs, out_specs=out_specs, check_vma=False)
```

```python
import functools

import jax
import jax.numpy as jnp
import ml_dtypes
import numpy as np
from jax import lax
from jax.experimental import pallas as pl
from jax.experimental.pallas import tpu as pltpu
from jax.sharding import PartitionSpec as P

GROUP = 8
BLOCK = 256
ROWS = 16
LANES = 128
AHEAD = 3


def dft_table(length):
    channel = np.arange(length) // 2
    phase = channel[:, None] * np.arange(length)[None, :] % length
    angles = phase * (2.0 * np.pi / length)
    real = (np.arange(length) % 2 == 0)[:, None]
    values = np.where(real, np.cos(angles), -np.sin(angles)) / np.sqrt(length)
    return (values.astype(ml_dtypes.bfloat16).astype(np.float32) / 8.0).astype(ml_dtypes.bfloat16)


def edge_frames(frames):
    return [*range(AHEAD, GROUP), *range(frames, frames + AHEAD)]


def tails_kernel(samples_ref, last_ref, first_ref, last, first, sems):
    count = samples_ref.shape[1]
    copies = [
        pltpu.make_async_copy(
            samples_ref.at[:, pl.ds(count - last.shape[1], last.shape[1])], last, sems.at[0]
        ),
        pltpu.make_async_copy(samples_ref.at[:, pl.ds(0, first.shape[1])], first, sems.at[1]),
    ]
    for copy in copies:
        copy.start()
    for copy, source, target in zip(copies, (last, first), (last_ref, first_ref), strict=True):
        copy.wait()
        target[...] = source[...].astype(jnp.float32).astype(jnp.bfloat16)


def transform_pair(filt, f, table_ref, spread):
    frames, inputs, fft = filt.shape
    pair = filt[f : f + 2].reshape(2 * inputs, fft)
    spectra = lax.dot_general(
        table_ref[...], pair, (((1,), (1,)), ((), ())), preferred_element_type=jnp.float32
    )
    spread[pl.ds(f, fft, stride=frames), :] = spectra[:, :inputs]
    spread[pl.ds(f + 1, fft, stride=frames), :] = spectra[:, inputs:]


def pack(spread, spectra_ref, group, part, parts):
    rows, _, inputs = spectra_ref.shape
    count = rows // parts
    block = spread[part * count * GROUP : (part + 1) * count * GROUP, :]
    where = (slice(part * count, (part + 1) * count), slice(group * GROUP, (group + 1) * GROUP))
    spectra_ref[where] = block.reshape(count, GROUP, inputs).astype(jnp.bfloat16)


def own_kernel(
    samples_ref, coef_hbm, table_hbm, spectra_ref, partial_ref,
    coef_ref, table_ref, held, filts, spreads, sems,
):
    taps, fft = coef_ref.shape
    inputs, count = held.shape
    frames = count // fft
    groups = frames // GROUP
    span = GROUP * fft
    edge = edge_frames(frames)
    pairs = GROUP // 2
    chunk = inputs // pairs

    boxes = [(slice(k * chunk, (k + 1) * chunk), slice(0, 2 * span)) for k in range(pairs)]
    boxes += [(slice(0, inputs), slice(g * span, (g + 1) * span)) for g in range(2, groups)]
    loads = [
        pltpu.make_async_copy(
            samples_ref.at[pl.ds(r.start, r.stop - r.start), pl.ds(c.start, c.stop - c.start)],
            held.at[pl.ds(r.start, r.stop - r.start), pl.ds(c.start, c.stop - c.start)],
            sems.at[k],
        )
        for k, (r, c) in enumerate(boxes)
    ]
    coef_copy = pltpu.make_async_copy(coef_hbm, coef_ref, sems.at[len(loads)])
    table_copy = pltpu.make_async_copy(table_hbm, table_ref, sems.at[len(loads) + 1])
    coef_copy.start()
    for load in loads[:3]:
        load.start()
    table_copy.start()

    def arrive(k):
        loads[k].wait()
        if k + 3 < len(loads):
            loads[k + 3].start()

    def filter_rows(g, i):
        rows = slice(i, i + ROWS)
        for n in range(0, fft, LANES):
            coefs = [coef_ref[p : p + 1, n : n + LANES] for p in range(taps)]

            def frame(f):
                return held[rows, f * fft + n : f * fft + n + LANES].astype(jnp.float32)

            def share(f, known):
                total = None
                for p in range(taps):
                    if f - p in known:
                        term = coefs[p] * known[f - p]
                        total = term if total is None else total + term
                return total

            if g == 0:
                known = {f: frame(f) for f in range(GROUP)}
                for slot, f in enumerate(edge[:-AHEAD]):
                    partial_ref[slot, rows, n : n + LANES] = share(f, known)
                known = {f: frame(f) for f in range(frames + 1 - taps, frames)}
                for slot, f in enumerate(edge[-AHEAD:]):
                    partial_ref[slot + GROUP - AHEAD, rows, n : n + LANES] = share(f, known)
            else:
                known = {f: frame(f) for f in range(g * GROUP + 1 - taps, g * GROUP)}
                for slot in range(GROUP):
                    f = g * GROUP + slot
                    known[f] = frame(f)
                    filts[g % 2][slot, rows, n : n + LANES] = share(f, known).astype(jnp.bfloat16)

    coef_copy.wait()
    for g in range(1, groups):
        if g == 2:
            table_copy.wait()
        if g >= 2:
            arrive(pairs + g - 2)
        for pair in range(pairs):
            if g >= 2:
                transform_pair(filts[(g - 1) % 2], 2 * pair, table_ref, spreads[(g - 1) % 2])
            if g >= 3:
                pack(spreads[g % 2], spectra_ref, g - 2, pair, pairs)
            if g == 1:
                arrive(pair)
            for i in range(pair * chunk, (pair + 1) * chunk, ROWS):
                filter_rows(g, i)
    last = groups - 1
    for pair in range(pairs):
        transform_pair(filts[last % 2], 2 * pair, table_ref, spreads[last % 2])
        pack(spreads[(last - 1) % 2], spectra_ref, last - 1, pair, pairs)
        filter_rows(0, pair * 2 * ROWS)
        filter_rows(0, pair * 2 * ROWS + ROWS)
    pack(spreads[last % 2], spectra_ref, last, 0, 1)


def edge_kernel(
    has_behind_ref, has_own_ref, behind_ref, ahead_ref, partial_ref, coef_ref, table_ref, _, spectra_ref,
    masked_ref, filt, spread, *, frames,
):
    taps, fft = coef_ref.shape
    inputs = behind_ref.shape[0]
    past = behind_ref.shape[1] // fft
    has_own = has_own_ref[0]
    edge = edge_frames(frames)
    masked_ref[...] = coef_ref[...] * has_behind_ref[0]

    for slot in range(0, GROUP, 2):
        for i in range(0, inputs, ROWS):
            rows = slice(i, i + ROWS)
            for n in range(0, fft, LANES):
                lanes = slice(n, n + LANES)
                samples = {}

                def frame(f):
                    if f not in samples:
                        ref, k = (behind_ref, f + past) if f < 0 else (ahead_ref, f - frames)
                        value = ref[rows, k * fft + n : k * fft + n + LANES]
                        samples[f] = value.astype(jnp.float32)
                    return samples[f]

                for s in (slot, slot + 1):
                    f = edge[s]
                    value = partial_ref[s, rows, lanes]
                    if f < frames:
                        for p in range(f + 1, taps):
                            value = value + masked_ref[p : p + 1, lanes] * frame(f - p)
                    else:
                        value = value * has_own
                        for p in range(f - frames + 1):
                            value = value + coef_ref[p : p + 1, lanes] * frame(f - p)
                    filt[s, rows, lanes] = value.astype(jnp.bfloat16)
        transform_pair(filt, slot, table_ref, spread)
    pack(spread, spectra_ref, 0, 0, 1)


def correlate_kernel(recv_ref, out_ref, held, turned, swapped, stage, sems):
    tm_count, input_count, items, _, frames, inputs = recv_ref.shape
    half = tm_count * frames
    width = input_count * inputs
    scale = 1.0 / half
    copies = []

    def give(c, part, i, j, value):
        rows, cols = pl.ds(i, BLOCK), pl.ds(j, BLOCK)
        stage[c, part, rows, cols] = value.astype(jnp.bfloat16)
        copy = pltpu.make_async_copy(
            stage.at[c, part, rows, cols], out_ref.at[c, part, rows, cols], sems.at[len(copies)]
        )
        copy.start()
        copies.append(copy)

    for c in range(items):
        for r in range(2):
            for a in range(tm_count):
                for b in range(input_count):
                    rows = slice(r * half + a * frames, r * half + (a + 1) * frames)
                    cols = slice(b * inputs, (b + 1) * inputs)
                    held[c, rows, cols] = recv_ref[a, b, c, r]
        turned[c] = held[c].T
        swapped[c, :half] = -held[c, half:]
        swapped[c, half:] = held[c, :half]
        for i in range(0, width, BLOCK):
            for j in range(i, width, BLOCK):
                left = turned[c, i : i + BLOCK]
                real = scale * jnp.dot(
                    left, held[c, :, j : j + BLOCK], preferred_element_type=jnp.float32
                )
                if j > i:
                    imag = scale * jnp.dot(
                        left, swapped[c, :, j : j + BLOCK], preferred_element_type=jnp.float32
                    )
                else:
                    cross = scale * jnp.dot(
                        turned[c, i : i + BLOCK, half:],
                        held[c, :half, j : j + BLOCK],
                        preferred_element_type=jnp.float32,
                    )
                    imag = cross - cross.T
                give(c, 0, i, j, real)
                give(c, 1, i, j, imag)
                if j > i:
                    give(c, 0, j, i, real.T)
                    give(c, 1, j, i, -imag.T)
    for copy in copies:
        copy.wait()


def local(samples, coefficients):
    inputs, sample_count = samples.shape
    taps, fft = coefficients.shape
    frames = sample_count // fft
    tm_count = lax.axis_size("tm")
    input_count = lax.axis_size("input")
    devices = tm_count * input_count
    groups = frames // GROUP
    past = (taps - 1 - AHEAD) * fft
    ahead = AHEAD * fft
    table = jnp.asarray(dft_table(fft))
    vmem = pl.BlockSpec(memory_space=pltpu.VMEM)
    smem = pl.BlockSpec(memory_space=pltpu.SMEM)
    hbm = pl.BlockSpec(memory_space=pltpu.HBM)

    ring = [(i, (i + 1) % tm_count) for i in range(tm_count)]
    own_tm = lax.axis_index("tm")
    has_behind = jnp.where(own_tm > 0, 1.0, 0.0).astype(jnp.float32).reshape(1)
    has_own = jnp.where(own_tm < tm_count - 1, 1.0, 0.0).astype(jnp.float32).reshape(1)
    spectra_type = pltpu.VMEM((fft, frames, inputs), jnp.bfloat16)
    in_hbm = lambda array: pltpu.with_memory_space_constraint(array, pltpu.HBM)
    filt = pltpu.VMEM((GROUP, inputs, fft), jnp.bfloat16)
    spread = pltpu.VMEM((fft * GROUP, inputs), jnp.float32)
    last, first = pl.pallas_call(
        tails_kernel,
        in_specs=[hbm],
        out_specs=[vmem, vmem],
        out_shape=[
            pltpu.VMEM((inputs, past), jnp.bfloat16),
            pltpu.VMEM((inputs, ahead), jnp.bfloat16),
        ],
        scratch_shapes=[
            pltpu.VMEM((inputs, past), jnp.int32),
            pltpu.VMEM((inputs, ahead), jnp.int32),
            pltpu.SemaphoreType.DMA((2,)),
        ],
        compiler_params=pltpu.CompilerParams(vmem_limit_bytes=8 << 20),
        name="tails",
    )(in_hbm(samples))
    from_behind = lax.ppermute(last, "tm", ring)
    from_ahead = lax.ppermute(first, "tm", [(b, a) for a, b in ring])

    spectra, partial = pl.pallas_call(
        own_kernel,
        in_specs=[hbm, hbm, hbm],
        out_specs=[vmem, vmem],
        out_shape=[spectra_type, pltpu.VMEM((GROUP, inputs, fft), jnp.float32)],
        scratch_shapes=[
            pltpu.VMEM((taps, fft), jnp.float32),
            pltpu.VMEM((fft, fft), jnp.bfloat16),
            pltpu.VMEM((inputs, sample_count), jnp.int32),
            [filt, filt],
            [spread, spread],
            pltpu.SemaphoreType.DMA((GROUP // 2 + groups,)),
        ],
        compiler_params=pltpu.CompilerParams(vmem_limit_bytes=24 << 20),
        name="own_frames",
    )(in_hbm(samples), in_hbm(coefficients), in_hbm(table))
    spectra = pl.pallas_call(
        functools.partial(edge_kernel, frames=frames),
        in_specs=[smem] * 2 + [vmem] * 6,
        out_specs=vmem,
        out_shape=spectra_type,
        scratch_shapes=[
            pltpu.VMEM((taps, fft), jnp.float32),
            filt,
            spread,
        ],
        input_output_aliases={7: 0},
        compiler_params=pltpu.CompilerParams(vmem_limit_bytes=16 << 20),
        name="edge_frames",
    )(has_behind, has_own, from_behind, from_ahead, partial, coefficients, table, spectra)

    items = fft // (2 * devices)
    outgoing = spectra.reshape(devices, 2 * items, frames, inputs)
    received = lax.all_to_all(outgoing, ("tm", "input"), 0, 0, tiled=True)
    received = received.reshape(tm_count, input_count, items, 2, frames, inputs)
    depth = 2 * tm_count * frames
    width = input_count * inputs
    blocks = (width // BLOCK) ** 2
    return pl.pallas_call(
        correlate_kernel,
        in_specs=[vmem],
        out_specs=hbm,
        out_shape=jax.ShapeDtypeStruct((items, 2, width, width), jnp.bfloat16),
        scratch_shapes=[
            pltpu.VMEM((items, depth, width), jnp.bfloat16),
            pltpu.VMEM((items, width, depth), jnp.bfloat16),
            pltpu.VMEM((items, depth, width), jnp.bfloat16),
            pltpu.VMEM((items, 2, width, width), jnp.bfloat16),
            pltpu.SemaphoreType.DMA((2 * items * blocks,)),
        ],
        compiler_params=pltpu.CompilerParams(vmem_limit_bytes=36 << 20),
        name="correlate",
    )(received)


def solution(mesh):
    in_specs = (P("input", "tm"), P())
    out_specs = P(("tm", "input"), None, None, None)
    return jax.shard_map(local, mesh=mesh, in_specs=in_specs, out_specs=out_specs, check_vma=False)
```

```python
import functools

import jax
import jax.numpy as jnp
import ml_dtypes
import numpy as np
from jax import lax
from jax.experimental import pallas as pl
from jax.experimental.pallas import tpu as pltpu
from jax.sharding import PartitionSpec as P

GROUP = 8
BLOCK = 256
ROWS = 16
LANES = 128
AHEAD = 2


def dft_table(length):
    channel = np.arange(length) // 2
    phase = channel[:, None] * np.arange(length)[None, :] % length
    angles = phase * (2.0 * np.pi / length)
    real = (np.arange(length) % 2 == 0)[:, None]
    values = np.where(real, np.cos(angles), -np.sin(angles)) / np.sqrt(length)
    return (values.astype(ml_dtypes.bfloat16).astype(np.float32) / 8.0).astype(ml_dtypes.bfloat16)


def edge_frames(frames):
    return [*range(AHEAD, GROUP), *range(frames, frames + AHEAD)]


def tails_kernel(samples_ref, last_ref, first_ref, last, first, sems):
    count = samples_ref.shape[1]
    copies = [
        pltpu.make_async_copy(
            samples_ref.at[:, pl.ds(count - last.shape[1], last.shape[1])], last, sems.at[0]
        ),
        pltpu.make_async_copy(samples_ref.at[:, pl.ds(0, first.shape[1])], first, sems.at[1]),
    ]
    for copy in copies:
        copy.start()
    for copy, source, target in zip(copies, (last, first), (last_ref, first_ref), strict=True):
        copy.wait()
        target[...] = source[...].astype(jnp.float32).astype(jnp.bfloat16)


def transform_pair(filt, f, table_ref, spread):
    frames, inputs, fft = filt.shape
    pair = filt[f : f + 2].reshape(2 * inputs, fft)
    spectra = lax.dot_general(
        table_ref[...], pair, (((1,), (1,)), ((), ())), preferred_element_type=jnp.float32
    )
    spread[pl.ds(f, fft, stride=frames), :] = spectra[:, :inputs]
    spread[pl.ds(f + 1, fft, stride=frames), :] = spectra[:, inputs:]


def pack(spread, spectra_ref, group, part, parts):
    rows, _, inputs = spectra_ref.shape
    count = rows // parts
    block = spread[part * count * GROUP : (part + 1) * count * GROUP, :]
    where = (slice(part * count, (part + 1) * count), slice(group * GROUP, (group + 1) * GROUP))
    spectra_ref[where] = block.reshape(count, GROUP, inputs).astype(jnp.bfloat16)


def own_kernel(
    samples_ref, coef_hbm, table_hbm, spectra_ref, partial_ref,
    coef_ref, table_ref, held, filts, spreads, sems,
):
    taps, fft = coef_ref.shape
    inputs, count = held.shape
    frames = count // fft
    groups = frames // GROUP
    span = GROUP * fft
    edge = edge_frames(frames)
    pairs = GROUP // 2
    chunk = inputs // pairs

    boxes = [(slice(k * chunk, (k + 1) * chunk), slice(0, 2 * span)) for k in range(pairs)]
    boxes += [(slice(0, inputs), slice(g * span, (g + 1) * span)) for g in range(2, groups)]
    loads = [
        pltpu.make_async_copy(
            samples_ref.at[pl.ds(r.start, r.stop - r.start), pl.ds(c.start, c.stop - c.start)],
            held.at[pl.ds(r.start, r.stop - r.start), pl.ds(c.start, c.stop - c.start)],
            sems.at[k],
        )
        for k, (r, c) in enumerate(boxes)
    ]
    coef_copy = pltpu.make_async_copy(coef_hbm, coef_ref, sems.at[len(loads)])
    table_copy = pltpu.make_async_copy(table_hbm, table_ref, sems.at[len(loads) + 1])
    coef_copy.start()
    for load in loads[:3]:
        load.start()
    table_copy.start()

    def arrive(k):
        loads[k].wait()
        if k + 3 < len(loads):
            loads[k + 3].start()

    def filter_rows(g, i):
        rows = slice(i, i + ROWS)
        for n in range(0, fft, LANES):
            coefs = [coef_ref[p : p + 1, n : n + LANES] for p in range(taps)]

            def frame(f):
                return held[rows, f * fft + n : f * fft + n + LANES].astype(jnp.float32)

            def share(f, known):
                total = None
                for p in range(taps):
                    if f - p in known:
                        term = coefs[p] * known[f - p]
                        total = term if total is None else total + term
                return total

            if g == 0:
                known = {f: frame(f) for f in range(GROUP)}
                for slot, f in enumerate(edge[:-AHEAD]):
                    partial_ref[slot, rows, n : n + LANES] = share(f, known)
                known = {f: frame(f) for f in range(frames + 1 - taps, frames)}
                for slot, f in enumerate(edge[-AHEAD:]):
                    partial_ref[slot + GROUP - AHEAD, rows, n : n + LANES] = share(f, known)
            else:
                known = {f: frame(f) for f in range(g * GROUP + 1 - taps, g * GROUP)}
                for slot in range(GROUP):
                    f = g * GROUP + slot
                    known[f] = frame(f)
                    filts[g % 2][slot, rows, n : n + LANES] = share(f, known).astype(jnp.bfloat16)

    coef_copy.wait()
    for g in range(1, groups):
        if g == 2:
            table_copy.wait()
        if g >= 2:
            arrive(pairs + g - 2)
        for pair in range(pairs):
            if g >= 2:
                transform_pair(filts[(g - 1) % 2], 2 * pair, table_ref, spreads[(g - 1) % 2])
            if g >= 3:
                pack(spreads[g % 2], spectra_ref, g - 2, pair, pairs)
            if g == 1:
                arrive(pair)
            for i in range(pair * chunk, (pair + 1) * chunk, ROWS):
                filter_rows(g, i)
    last = groups - 1
    for pair in range(pairs):
        transform_pair(filts[last % 2], 2 * pair, table_ref, spreads[last % 2])
        pack(spreads[(last - 1) % 2], spectra_ref, last - 1, pair, pairs)
        filter_rows(0, pair * 2 * ROWS)
        filter_rows(0, pair * 2 * ROWS + ROWS)
    pack(spreads[last % 2], spectra_ref, last, 0, 1)


def edge_kernel(
    has_behind_ref, has_own_ref, behind_ref, ahead_ref, partial_ref, coef_ref, table_ref, _, spectra_ref,
    masked_ref, filt, spread, *, frames,
):
    taps, fft = coef_ref.shape
    inputs = behind_ref.shape[0]
    past = behind_ref.shape[1] // fft
    has_own = has_own_ref[0]
    edge = edge_frames(frames)
    masked_ref[...] = coef_ref[...] * has_behind_ref[0]

    for slot in range(0, GROUP, 2):
        for i in range(0, inputs, ROWS):
            rows = slice(i, i + ROWS)
            for n in range(0, fft, LANES):
                lanes = slice(n, n + LANES)
                samples = {}

                def frame(f):
                    if f not in samples:
                        ref, k = (behind_ref, f + past) if f < 0 else (ahead_ref, f - frames)
                        value = ref[rows, k * fft + n : k * fft + n + LANES]
                        samples[f] = value.astype(jnp.float32)
                    return samples[f]

                for s in (slot, slot + 1):
                    f = edge[s]
                    value = partial_ref[s, rows, lanes]
                    if f < frames:
                        for p in range(f + 1, taps):
                            value = value + masked_ref[p : p + 1, lanes] * frame(f - p)
                    else:
                        value = value * has_own
                        for p in range(f - frames + 1):
                            value = value + coef_ref[p : p + 1, lanes] * frame(f - p)
                    filt[s, rows, lanes] = value.astype(jnp.bfloat16)
        transform_pair(filt, slot, table_ref, spread)
    pack(spread, spectra_ref, 0, 0, 1)


def correlate_kernel(recv_ref, out_ref, held, turned, swapped, stage, sems):
    tm_count, input_count, items, _, frames, inputs = recv_ref.shape
    half = tm_count * frames
    width = input_count * inputs
    scale = 1.0 / half
    copies = []

    def give(c, part, i, j, value):
        rows, cols = pl.ds(i, BLOCK), pl.ds(j, BLOCK)
        stage[c, part, rows, cols] = value.astype(jnp.bfloat16)
        copy = pltpu.make_async_copy(
            stage.at[c, part, rows, cols], out_ref.at[c, part, rows, cols], sems.at[len(copies)]
        )
        copy.start()
        copies.append(copy)

    for c in range(items):
        for r in range(2):
            for a in range(tm_count):
                for b in range(input_count):
                    rows = slice(r * half + a * frames, r * half + (a + 1) * frames)
                    cols = slice(b * inputs, (b + 1) * inputs)
                    held[c, rows, cols] = recv_ref[a, b, c, r]
        turned[c] = held[c].T
        swapped[c, :half] = -held[c, half:]
        swapped[c, half:] = held[c, :half]
        for i in range(0, width, BLOCK):
            for j in range(i, width, BLOCK):
                left = turned[c, i : i + BLOCK]
                real = scale * jnp.dot(
                    left, held[c, :, j : j + BLOCK], preferred_element_type=jnp.float32
                )
                if j > i:
                    imag = scale * jnp.dot(
                        left, swapped[c, :, j : j + BLOCK], preferred_element_type=jnp.float32
                    )
                else:
                    cross = scale * jnp.dot(
                        turned[c, i : i + BLOCK, half:],
                        held[c, :half, j : j + BLOCK],
                        preferred_element_type=jnp.float32,
                    )
                    imag = cross - cross.T
                give(c, 0, i, j, real)
                give(c, 1, i, j, imag)
                if j > i:
                    give(c, 0, j, i, real.T)
                    give(c, 1, j, i, -imag.T)
    for copy in copies:
        copy.wait()


def local(samples, coefficients):
    inputs, sample_count = samples.shape
    taps, fft = coefficients.shape
    frames = sample_count // fft
    tm_count = lax.axis_size("tm")
    input_count = lax.axis_size("input")
    devices = tm_count * input_count
    groups = frames // GROUP
    past = (taps - 1 - AHEAD) * fft
    ahead = AHEAD * fft
    table = jnp.asarray(dft_table(fft))
    vmem = pl.BlockSpec(memory_space=pltpu.VMEM)
    smem = pl.BlockSpec(memory_space=pltpu.SMEM)
    hbm = pl.BlockSpec(memory_space=pltpu.HBM)

    ring = [(i, (i + 1) % tm_count) for i in range(tm_count)]
    own_tm = lax.axis_index("tm")
    has_behind = jnp.where(own_tm > 0, 1.0, 0.0).astype(jnp.float32).reshape(1)
    has_own = jnp.where(own_tm < tm_count - 1, 1.0, 0.0).astype(jnp.float32).reshape(1)
    spectra_type = pltpu.VMEM((fft, frames, inputs), jnp.bfloat16)
    in_hbm = lambda array: pltpu.with_memory_space_constraint(array, pltpu.HBM)
    filt = pltpu.VMEM((GROUP, inputs, fft), jnp.bfloat16)
    spread = pltpu.VMEM((fft * GROUP, inputs), jnp.float32)
    last, first = pl.pallas_call(
        tails_kernel,
        in_specs=[hbm],
        out_specs=[vmem, vmem],
        out_shape=[
            pltpu.VMEM((inputs, past), jnp.bfloat16),
            pltpu.VMEM((inputs, ahead), jnp.bfloat16),
        ],
        scratch_shapes=[
            pltpu.VMEM((inputs, past), jnp.int32),
            pltpu.VMEM((inputs, ahead), jnp.int32),
            pltpu.SemaphoreType.DMA((2,)),
        ],
        compiler_params=pltpu.CompilerParams(vmem_limit_bytes=8 << 20),
        name="tails",
    )(in_hbm(samples))
    from_behind = lax.ppermute(last, "tm", ring)
    from_ahead = lax.ppermute(first, "tm", [(b, a) for a, b in ring])

    spectra, partial = pl.pallas_call(
        own_kernel,
        in_specs=[hbm, hbm, hbm],
        out_specs=[vmem, vmem],
        out_shape=[spectra_type, pltpu.VMEM((GROUP, inputs, fft), jnp.float32)],
        scratch_shapes=[
            pltpu.VMEM((taps, fft), jnp.float32),
            pltpu.VMEM((fft, fft), jnp.bfloat16),
            pltpu.VMEM((inputs, sample_count), jnp.int32),
            [filt, filt],
            [spread, spread],
            pltpu.SemaphoreType.DMA((GROUP // 2 + groups,)),
        ],
        compiler_params=pltpu.CompilerParams(vmem_limit_bytes=24 << 20),
        name="own_frames",
    )(in_hbm(samples), in_hbm(coefficients), in_hbm(table))
    spectra = pl.pallas_call(
        functools.partial(edge_kernel, frames=frames),
        in_specs=[smem] * 2 + [vmem] * 6,
        out_specs=vmem,
        out_shape=spectra_type,
        scratch_shapes=[
            pltpu.VMEM((taps, fft), jnp.float32),
            filt,
            spread,
        ],
        input_output_aliases={7: 0},
        compiler_params=pltpu.CompilerParams(vmem_limit_bytes=16 << 20),
        name="edge_frames",
    )(has_behind, has_own, from_behind, from_ahead, partial, coefficients, table, spectra)

    items = fft // (2 * devices)
    outgoing = spectra.reshape(devices, 2 * items, frames, inputs)
    received = lax.all_to_all(outgoing, ("tm", "input"), 0, 0, tiled=True)
    received = received.reshape(tm_count, input_count, items, 2, frames, inputs)
    depth = 2 * tm_count * frames
    width = input_count * inputs
    blocks = (width // BLOCK) ** 2
    return pl.pallas_call(
        correlate_kernel,
        in_specs=[vmem],
        out_specs=hbm,
        out_shape=jax.ShapeDtypeStruct((items, 2, width, width), jnp.bfloat16),
        scratch_shapes=[
            pltpu.VMEM((items, depth, width), jnp.bfloat16),
            pltpu.VMEM((items, width, depth), jnp.bfloat16),
            pltpu.VMEM((items, depth, width), jnp.bfloat16),
            pltpu.VMEM((items, 2, width, width), jnp.bfloat16),
            pltpu.SemaphoreType.DMA((2 * items * blocks,)),
        ],
        compiler_params=pltpu.CompilerParams(vmem_limit_bytes=36 << 20),
        name="correlate",
    )(received)


def solution(mesh):
    in_specs = (P("input", "tm"), P())
    out_specs = P(("tm", "input"), None, None, None)
    return jax.shard_map(local, mesh=mesh, in_specs=in_specs, out_specs=out_specs, check_vma=False)
```

```python
import functools

import jax
import jax.numpy as jnp
import ml_dtypes
import numpy as np
from jax import lax
from jax.experimental import pallas as pl
from jax.experimental.pallas import tpu as pltpu
from jax.sharding import PartitionSpec as P

GROUP = 8
BLOCK = 256
ROWS = 16
LANES = 128
AHEAD = 2


def dft_table(length):
    channel = np.arange(length) // 2
    phase = channel[:, None] * np.arange(length)[None, :] % length
    angles = phase * (2.0 * np.pi / length)
    real = (np.arange(length) % 2 == 0)[:, None]
    values = np.where(real, np.cos(angles), -np.sin(angles)) / np.sqrt(length)
    return (values.astype(ml_dtypes.bfloat16).astype(np.float32) / 8.0).astype(ml_dtypes.bfloat16)


def edge_frames(frames):
    return [*range(AHEAD, GROUP), *range(frames, frames + AHEAD)]


def tails_kernel(samples_ref, last_ref, first_ref, last, first, sems):
    inputs, count = samples_ref.shape
    parts = sems.shape[0] // 2
    step = inputs // parts
    copies = []
    for part in range(parts):
        rows = pl.ds(part * step, step)
        for held, target, start in ((last, last_ref, count - last.shape[1]), (first, first_ref, 0)):
            source = samples_ref.at[rows, pl.ds(start, held.shape[1])]
            copy = pltpu.make_async_copy(source, held.at[rows], sems.at[len(copies)])
            copy.start()
            copies.append((copy, slice(part * step, (part + 1) * step), held, target))
    for copy, rows, held, target in copies:
        copy.wait()
        target[rows] = held[rows].astype(jnp.float32).astype(jnp.bfloat16)


def transform_pair(filt, f, table_ref, spread):
    frames, inputs, fft = filt.shape
    pair = filt[f : f + 2].reshape(2 * inputs, fft)
    spectra = lax.dot_general(
        table_ref[...], pair, (((1,), (1,)), ((), ())), preferred_element_type=jnp.float32
    )
    spread[pl.ds(f, fft, stride=frames), :] = spectra[:, :inputs]
    spread[pl.ds(f + 1, fft, stride=frames), :] = spectra[:, inputs:]


def pack(spread, spectra_ref, group, part, parts):
    rows, _, inputs = spectra_ref.shape
    count = rows // parts
    block = spread[part * count * GROUP : (part + 1) * count * GROUP, :]
    where = (slice(part * count, (part + 1) * count), slice(group * GROUP, (group + 1) * GROUP))
    spectra_ref[where] = block.reshape(count, GROUP, inputs).astype(jnp.bfloat16)


def own_kernel(
    samples_ref, coef_hbm, table_hbm, spectra_ref, partial_ref,
    coef_ref, table_ref, held, filts, spreads, sems,
):
    taps, fft = coef_ref.shape
    inputs, count = held.shape
    frames = count // fft
    groups = frames // GROUP
    span = GROUP * fft
    edge = edge_frames(frames)
    pairs = GROUP // 2
    chunk = inputs // pairs

    boxes = [(slice(k * chunk, (k + 1) * chunk), slice(0, 2 * span)) for k in range(pairs)]
    boxes += [(slice(0, inputs), slice(g * span, (g + 1) * span)) for g in range(2, groups)]
    loads = [
        pltpu.make_async_copy(
            samples_ref.at[pl.ds(r.start, r.stop - r.start), pl.ds(c.start, c.stop - c.start)],
            held.at[pl.ds(r.start, r.stop - r.start), pl.ds(c.start, c.stop - c.start)],
            sems.at[k],
        )
        for k, (r, c) in enumerate(boxes)
    ]
    coef_copy = pltpu.make_async_copy(coef_hbm, coef_ref, sems.at[len(loads)])
    table_copy = pltpu.make_async_copy(table_hbm, table_ref, sems.at[len(loads) + 1])
    coef_copy.start()
    for load in loads[:3]:
        load.start()
    table_copy.start()

    def arrive(k):
        loads[k].wait()
        if k + 3 < len(loads):
            loads[k + 3].start()

    def filter_rows(g, i):
        rows = slice(i, i + ROWS)
        for n in range(0, fft, LANES):
            coefs = [coef_ref[p : p + 1, n : n + LANES] for p in range(taps)]

            def frame(f):
                return held[rows, f * fft + n : f * fft + n + LANES].astype(jnp.float32)

            def share(f, known):
                total = None
                for p in range(taps):
                    if f - p in known:
                        term = coefs[p] * known[f - p]
                        total = term if total is None else total + term
                return total

            if g == 0:
                known = {f: frame(f) for f in range(GROUP)}
                for slot, f in enumerate(edge[:-AHEAD]):
                    partial_ref[slot, rows, n : n + LANES] = share(f, known)
                known = {f: frame(f) for f in range(frames + 1 - taps, frames)}
                for slot, f in enumerate(edge[-AHEAD:]):
                    partial_ref[slot + GROUP - AHEAD, rows, n : n + LANES] = share(f, known)
            else:
                known = {f: frame(f) for f in range(g * GROUP + 1 - taps, g * GROUP)}
                for slot in range(GROUP):
                    f = g * GROUP + slot
                    known[f] = frame(f)
                    filts[g % 2][slot, rows, n : n + LANES] = share(f, known).astype(jnp.bfloat16)

    coef_copy.wait()
    for g in range(1, groups):
        if g == 2:
            table_copy.wait()
        if g >= 2:
            arrive(pairs + g - 2)
        for pair in range(pairs):
            if g >= 2:
                transform_pair(filts[(g - 1) % 2], 2 * pair, table_ref, spreads[(g - 1) % 2])
            if g >= 3:
                pack(spreads[g % 2], spectra_ref, g - 2, pair, pairs)
            if g == 1:
                arrive(pair)
            for i in range(pair * chunk, (pair + 1) * chunk, ROWS):
                filter_rows(g, i)
    last = groups - 1
    for pair in range(pairs):
        transform_pair(filts[last % 2], 2 * pair, table_ref, spreads[last % 2])
        pack(spreads[(last - 1) % 2], spectra_ref, last - 1, pair, pairs)
        filter_rows(0, pair * 2 * ROWS)
        filter_rows(0, pair * 2 * ROWS + ROWS)
    pack(spreads[last % 2], spectra_ref, last, 0, 1)


def edge_kernel(
    has_behind_ref, has_own_ref, behind_ref, ahead_ref, partial_ref, coef_ref, table_ref, _, spectra_ref,
    masked_ref, filt, spread, *, frames,
):
    taps, fft = coef_ref.shape
    inputs = behind_ref.shape[0]
    past = behind_ref.shape[1] // fft
    has_own = has_own_ref[0]
    edge = edge_frames(frames)
    masked_ref[...] = coef_ref[...] * has_behind_ref[0]

    for slot in range(0, GROUP, 2):
        for i in range(0, inputs, ROWS):
            rows = slice(i, i + ROWS)
            for n in range(0, fft, LANES):
                lanes = slice(n, n + LANES)
                samples = {}

                def frame(f):
                    if f not in samples:
                        ref, k = (behind_ref, f + past) if f < 0 else (ahead_ref, f - frames)
                        value = ref[rows, k * fft + n : k * fft + n + LANES]
                        samples[f] = value.astype(jnp.float32)
                    return samples[f]

                for s in (slot, slot + 1):
                    f = edge[s]
                    value = partial_ref[s, rows, lanes]
                    if f < frames:
                        for p in range(f + 1, taps):
                            value = value + masked_ref[p : p + 1, lanes] * frame(f - p)
                    else:
                        value = value * has_own
                        for p in range(f - frames + 1):
                            value = value + coef_ref[p : p + 1, lanes] * frame(f - p)
                    filt[s, rows, lanes] = value.astype(jnp.bfloat16)
        transform_pair(filt, slot, table_ref, spread)
    pack(spread, spectra_ref, 0, 0, 1)


def correlate_kernel(recv_ref, out_ref, held, turned, summed, less, stage, sems):
    tm_count, input_count, items, _, frames, inputs = recv_ref.shape
    half = tm_count * frames
    width = input_count * inputs
    scale = 1.0 / half
    copies = []

    def give(c, part, i, j, value):
        rows, cols = pl.ds(i, BLOCK), pl.ds(j, BLOCK)
        stage[c, part, rows, cols] = value
        copy = pltpu.make_async_copy(
            stage.at[c, part, rows, cols], out_ref.at[c, part, rows, cols], sems.at[len(copies)]
        )
        copy.start()
        copies.append(copy)

    def product(left, right):
        return scale * jnp.dot(left, right, preferred_element_type=jnp.float32)

    for c in range(items):
        for r in range(2):
            for a in range(tm_count):
                for b in range(input_count):
                    rows = slice(r * half + a * frames, r * half + (a + 1) * frames)
                    cols = slice(b * inputs, (b + 1) * inputs)
                    held[c, rows, cols] = recv_ref[a, b, c, r]
        turned[c] = held[c].T
        summed[c] = turned[c, :, :half] + turned[c, :, half:]
        less[c] = held[c, :half] - held[c, half:]
        for i in range(0, width, BLOCK):
            rows = slice(i, i + BLOCK)
            real = product(turned[c, rows], held[c, :, rows])
            cross = product(turned[c, rows, half:], held[c, :half, rows])
            give(c, 0, i, i, real.astype(jnp.bfloat16))
            give(c, 1, i, i, (cross - cross.T).astype(jnp.bfloat16))
            for j in range(i + BLOCK, width, BLOCK):
                cols = slice(j, j + BLOCK)
                first = product(turned[c, rows, :half], held[c, :half, cols])
                second = product(turned[c, rows, half:], held[c, half:, cols])
                mixed = product(summed[c, rows], less[c, :, cols])
                real = (first + second).astype(jnp.bfloat16)
                imag = (mixed - first + second).astype(jnp.bfloat16)
                give(c, 0, i, j, real)
                give(c, 1, i, j, imag)
                give(c, 0, j, i, real.T)
                give(c, 1, j, i, (-imag).T)
    for copy in copies:
        copy.wait()


def local(samples, coefficients):
    inputs, sample_count = samples.shape
    taps, fft = coefficients.shape
    frames = sample_count // fft
    tm_count = lax.axis_size("tm")
    input_count = lax.axis_size("input")
    devices = tm_count * input_count
    groups = frames // GROUP
    past = (taps - 1 - AHEAD) * fft
    ahead = AHEAD * fft
    table = jnp.asarray(dft_table(fft))
    vmem = pl.BlockSpec(memory_space=pltpu.VMEM)
    smem = pl.BlockSpec(memory_space=pltpu.SMEM)
    hbm = pl.BlockSpec(memory_space=pltpu.HBM)

    ring = [(i, (i + 1) % tm_count) for i in range(tm_count)]
    own_tm = lax.axis_index("tm")
    has_behind = jnp.where(own_tm > 0, 1.0, 0.0).astype(jnp.float32).reshape(1)
    has_own = jnp.where(own_tm < tm_count - 1, 1.0, 0.0).astype(jnp.float32).reshape(1)
    spectra_type = pltpu.VMEM((fft, frames, inputs), jnp.bfloat16)
    in_hbm = lambda array: pltpu.with_memory_space_constraint(array, pltpu.HBM)
    filt = pltpu.VMEM((GROUP, inputs, fft), jnp.bfloat16)
    spread = pltpu.VMEM((fft * GROUP, inputs), jnp.float32)
    last, first = pl.pallas_call(
        tails_kernel,
        in_specs=[hbm],
        out_specs=[vmem, vmem],
        out_shape=[
            pltpu.VMEM((inputs, past), jnp.bfloat16),
            pltpu.VMEM((inputs, ahead), jnp.bfloat16),
        ],
        scratch_shapes=[
            pltpu.VMEM((inputs, past), jnp.int32),
            pltpu.VMEM((inputs, ahead), jnp.int32),
            pltpu.SemaphoreType.DMA((8,)),
        ],
        compiler_params=pltpu.CompilerParams(vmem_limit_bytes=8 << 20),
        name="tails",
    )(in_hbm(samples))
    from_behind = lax.ppermute(last, "tm", ring)
    from_ahead = lax.ppermute(first, "tm", [(b, a) for a, b in ring])

    spectra, partial = pl.pallas_call(
        own_kernel,
        in_specs=[hbm, hbm, hbm],
        out_specs=[vmem, vmem],
        out_shape=[spectra_type, pltpu.VMEM((GROUP, inputs, fft), jnp.float32)],
        scratch_shapes=[
            pltpu.VMEM((taps, fft), jnp.float32),
            pltpu.VMEM((fft, fft), jnp.bfloat16),
            pltpu.VMEM((inputs, sample_count), jnp.int32),
            [filt, filt],
            [spread, spread],
            pltpu.SemaphoreType.DMA((GROUP // 2 + groups,)),
        ],
        compiler_params=pltpu.CompilerParams(vmem_limit_bytes=24 << 20),
        name="own_frames",
    )(in_hbm(samples), in_hbm(coefficients), in_hbm(table))
    spectra = pl.pallas_call(
        functools.partial(edge_kernel, frames=frames),
        in_specs=[smem] * 2 + [vmem] * 6,
        out_specs=vmem,
        out_shape=spectra_type,
        scratch_shapes=[
            pltpu.VMEM((taps, fft), jnp.float32),
            filt,
            spread,
        ],
        input_output_aliases={7: 0},
        compiler_params=pltpu.CompilerParams(vmem_limit_bytes=16 << 20),
        name="edge_frames",
    )(has_behind, has_own, from_behind, from_ahead, partial, coefficients, table, spectra)

    items = fft // (2 * devices)
    outgoing = spectra.reshape(devices, 2 * items, frames, inputs)
    received = lax.all_to_all(outgoing, ("tm", "input"), 0, 0, tiled=True)
    received = received.reshape(tm_count, input_count, items, 2, frames, inputs)
    depth = 2 * tm_count * frames
    width = input_count * inputs
    blocks = (width // BLOCK) ** 2
    return pl.pallas_call(
        correlate_kernel,
        in_specs=[vmem],
        out_specs=hbm,
        out_shape=jax.ShapeDtypeStruct((items, 2, width, width), jnp.bfloat16),
        scratch_shapes=[
            pltpu.VMEM((items, depth, width), jnp.bfloat16),
            pltpu.VMEM((items, width, depth), jnp.bfloat16),
            pltpu.VMEM((items, width, depth // 2), jnp.bfloat16),
            pltpu.VMEM((items, depth // 2, width), jnp.bfloat16),
            pltpu.VMEM((items, 2, width, width), jnp.bfloat16),
            pltpu.SemaphoreType.DMA((2 * items * blocks,)),
        ],
        compiler_params=pltpu.CompilerParams(vmem_limit_bytes=36 << 20),
        name="correlate",
    )(received)


def solution(mesh):
    in_specs = (P("input", "tm"), P())
    out_specs = P(("tm", "input"), None, None, None)
    return jax.shard_map(local, mesh=mesh, in_specs=in_specs, out_specs=out_specs, check_vma=False)
```

```python
import functools

import jax
import jax.numpy as jnp
import ml_dtypes
import numpy as np
from jax import lax
from jax.experimental import pallas as pl
from jax.experimental.pallas import tpu as pltpu
from jax.sharding import PartitionSpec as P

GROUP = 8
BLOCK = 256
ROWS = 16
LANES = 128
AHEAD = 2


def dft_table(length):
    channel = np.arange(length) // 2
    phase = channel[:, None] * np.arange(length)[None, :] % length
    angles = phase * (2.0 * np.pi / length)
    real = (np.arange(length) % 2 == 0)[:, None]
    values = np.where(real, np.cos(angles), -np.sin(angles)) / np.sqrt(length)
    return (values.astype(ml_dtypes.bfloat16).astype(np.float32) / 8.0).astype(ml_dtypes.bfloat16)


def edge_frames(frames):
    return [*range(AHEAD, GROUP), *range(frames, frames + AHEAD)]


def tails_kernel(samples_ref, last_ref, first_ref, last, first, sems):
    count = samples_ref.shape[1]
    copies = [
        pltpu.make_async_copy(
            samples_ref.at[:, pl.ds(count - last.shape[1], last.shape[1])], last, sems.at[0]
        ),
        pltpu.make_async_copy(samples_ref.at[:, pl.ds(0, first.shape[1])], first, sems.at[1]),
    ]
    for copy in copies:
        copy.start()
    for copy, source, target in zip(copies, (last, first), (last_ref, first_ref), strict=True):
        copy.wait()
        target[...] = source[...].astype(jnp.float32).astype(jnp.bfloat16)


def transform_pair(filt, f, table_ref, spread):
    frames, inputs, fft = filt.shape
    pair = filt[f : f + 2].reshape(2 * inputs, fft)
    spectra = lax.dot_general(
        table_ref[...], pair, (((1,), (1,)), ((), ())), preferred_element_type=jnp.float32
    )
    spread[pl.ds(f, fft, stride=frames), :] = spectra[:, :inputs]
    spread[pl.ds(f + 1, fft, stride=frames), :] = spectra[:, inputs:]


def pack(spread, spectra_ref, group, part, parts):
    rows, _, inputs = spectra_ref.shape
    count = rows // parts
    block = spread[part * count * GROUP : (part + 1) * count * GROUP, :]
    where = (slice(part * count, (part + 1) * count), slice(group * GROUP, (group + 1) * GROUP))
    spectra_ref[where] = block.reshape(count, GROUP, inputs).astype(jnp.bfloat16)


def own_kernel(
    samples_ref, coef_hbm, table_hbm, spectra_ref, partial_ref,
    coef_ref, table_ref, held, filts, spreads, sems,
):
    taps, fft = coef_ref.shape
    inputs, count = held.shape
    frames = count // fft
    groups = frames // GROUP
    span = GROUP * fft
    edge = edge_frames(frames)
    pairs = GROUP // 2
    chunk = inputs // pairs

    boxes = [(slice(k * chunk, (k + 1) * chunk), slice(0, 2 * span)) for k in range(pairs)]
    boxes += [(slice(0, inputs), slice(g * span, (g + 1) * span)) for g in range(2, groups)]
    loads = [
        pltpu.make_async_copy(
            samples_ref.at[pl.ds(r.start, r.stop - r.start), pl.ds(c.start, c.stop - c.start)],
            held.at[pl.ds(r.start, r.stop - r.start), pl.ds(c.start, c.stop - c.start)],
            sems.at[k],
        )
        for k, (r, c) in enumerate(boxes)
    ]
    coef_copy = pltpu.make_async_copy(coef_hbm, coef_ref, sems.at[len(loads)])
    table_copy = pltpu.make_async_copy(table_hbm, table_ref, sems.at[len(loads) + 1])
    coef_copy.start()
    for load in loads[:3]:
        load.start()
    table_copy.start()

    def arrive(k):
        loads[k].wait()
        if k + 3 < len(loads):
            loads[k + 3].start()

    def filter_rows(g, i):
        rows = slice(i, i + ROWS)
        for n in range(0, fft, LANES):
            coefs = [coef_ref[p : p + 1, n : n + LANES] for p in range(taps)]

            def frame(f):
                return held[rows, f * fft + n : f * fft + n + LANES].astype(jnp.float32)

            def share(f, known):
                total = None
                for p in range(taps):
                    if f - p in known:
                        term = coefs[p] * known[f - p]
                        total = term if total is None else total + term
                return total

            if g == 0:
                known = {f: frame(f) for f in range(GROUP)}
                for slot, f in enumerate(edge[:-AHEAD]):
                    partial_ref[slot, rows, n : n + LANES] = share(f, known)
                known = {f: frame(f) for f in range(frames + 1 - taps, frames)}
                for slot, f in enumerate(edge[-AHEAD:]):
                    partial_ref[slot + GROUP - AHEAD, rows, n : n + LANES] = share(f, known)
            else:
                known = {f: frame(f) for f in range(g * GROUP + 1 - taps, g * GROUP)}
                for slot in range(GROUP):
                    f = g * GROUP + slot
                    known[f] = frame(f)
                    filts[g % 2][slot, rows, n : n + LANES] = share(f, known).astype(jnp.bfloat16)

    coef_copy.wait()
    for g in range(1, groups):
        if g == 2:
            table_copy.wait()
        if g >= 2:
            arrive(pairs + g - 2)
        for pair in range(pairs):
            if g >= 2:
                transform_pair(filts[(g - 1) % 2], 2 * pair, table_ref, spreads[(g - 1) % 2])
            if g >= 3:
                pack(spreads[g % 2], spectra_ref, g - 2, pair, pairs)
            if g == 1:
                arrive(pair)
            for i in range(pair * chunk, (pair + 1) * chunk, ROWS):
                filter_rows(g, i)
    last = groups - 1
    for pair in range(pairs):
        transform_pair(filts[last % 2], 2 * pair, table_ref, spreads[last % 2])
        pack(spreads[(last - 1) % 2], spectra_ref, last - 1, pair, pairs)
        filter_rows(0, pair * ROWS)
    for pair in range(pairs):
        pack(spreads[last % 2], spectra_ref, last, pair, pairs)
        filter_rows(0, (pairs + pair) * ROWS)


def edge_kernel(
    has_behind_ref, has_own_ref, behind_ref, ahead_ref, partial_ref, coef_ref, table_ref, _, spectra_ref,
    masked_ref, filt, spread, *, frames,
):
    taps, fft = coef_ref.shape
    inputs = behind_ref.shape[0]
    past = behind_ref.shape[1] // fft
    has_own = has_own_ref[0]
    edge = edge_frames(frames)
    masked_ref[...] = coef_ref[...] * has_behind_ref[0]

    for slot in range(0, GROUP, 2):
        for i in range(0, inputs, ROWS):
            rows = slice(i, i + ROWS)
            for n in range(0, fft, LANES):
                lanes = slice(n, n + LANES)
                samples = {}

                def frame(f):
                    if f not in samples:
                        ref, k = (behind_ref, f + past) if f < 0 else (ahead_ref, f - frames)
                        value = ref[rows, k * fft + n : k * fft + n + LANES]
                        samples[f] = value.astype(jnp.float32)
                    return samples[f]

                for s in (slot, slot + 1):
                    f = edge[s]
                    value = partial_ref[s, rows, lanes]
                    if f < frames:
                        for p in range(f + 1, taps):
                            value = value + masked_ref[p : p + 1, lanes] * frame(f - p)
                    else:
                        value = value * has_own
                        for p in range(f - frames + 1):
                            value = value + coef_ref[p : p + 1, lanes] * frame(f - p)
                    filt[s, rows, lanes] = value.astype(jnp.bfloat16)
        transform_pair(filt, slot, table_ref, spread)
    pack(spread, spectra_ref, 0, 0, 1)


def correlate_kernel(recv_ref, out_ref, held, turned, swapped, stage, sems):
    tm_count, input_count, items, _, frames, inputs = recv_ref.shape
    half = tm_count * frames
    width = input_count * inputs
    scale = 1.0 / half
    copies = []

    def give(c, part, i, j, value):
        rows, cols = pl.ds(i, BLOCK), pl.ds(j, BLOCK)
        stage[c, part, rows, cols] = value
        copy = pltpu.make_async_copy(
            stage.at[c, part, rows, cols], out_ref.at[c, part, rows, cols], sems.at[len(copies)]
        )
        copy.start()
        copies.append(copy)

    for c in range(items):
        for r in range(2):
            for a in range(tm_count):
                for b in range(input_count):
                    rows = slice(r * half + a * frames, r * half + (a + 1) * frames)
                    cols = slice(b * inputs, (b + 1) * inputs)
                    held[c, rows, cols] = recv_ref[a, b, c, r]
        turned[c] = held[c].T
        swapped[c, :half] = -held[c, half:]
        swapped[c, half:] = held[c, :half]
        for i in range(0, width, BLOCK):
            for j in range(i, width, BLOCK):
                left = turned[c, i : i + BLOCK]
                real = scale * jnp.dot(
                    left, held[c, :, j : j + BLOCK], preferred_element_type=jnp.float32
                )
                if j > i:
                    imag = scale * jnp.dot(
                        left, swapped[c, :, j : j + BLOCK], preferred_element_type=jnp.float32
                    )
                else:
                    cross = scale * jnp.dot(
                        turned[c, i : i + BLOCK, half:],
                        held[c, :half, j : j + BLOCK],
                        preferred_element_type=jnp.float32,
                    )
                    imag = cross - cross.T
                real = real.astype(jnp.bfloat16)
                imag = imag.astype(jnp.bfloat16)
                give(c, 0, i, j, real)
                give(c, 1, i, j, imag)
                if j > i:
                    give(c, 0, j, i, real.T)
                    give(c, 1, j, i, (-imag).T)
    for copy in copies:
        copy.wait()


def local(samples, coefficients):
    inputs, sample_count = samples.shape
    taps, fft = coefficients.shape
    frames = sample_count // fft
    tm_count = lax.axis_size("tm")
    input_count = lax.axis_size("input")
    devices = tm_count * input_count
    groups = frames // GROUP
    past = (taps - 1 - AHEAD) * fft
    ahead = AHEAD * fft
    table = jnp.asarray(dft_table(fft))
    vmem = pl.BlockSpec(memory_space=pltpu.VMEM)
    smem = pl.BlockSpec(memory_space=pltpu.SMEM)
    hbm = pl.BlockSpec(memory_space=pltpu.HBM)

    ring = [(i, (i + 1) % tm_count) for i in range(tm_count)]
    own_tm = lax.axis_index("tm")
    has_behind = jnp.where(own_tm > 0, 1.0, 0.0).astype(jnp.float32).reshape(1)
    has_own = jnp.where(own_tm < tm_count - 1, 1.0, 0.0).astype(jnp.float32).reshape(1)
    spectra_type = pltpu.VMEM((fft, frames, inputs), jnp.bfloat16)
    in_hbm = lambda array: pltpu.with_memory_space_constraint(array, pltpu.HBM)
    filt = pltpu.VMEM((GROUP, inputs, fft), jnp.bfloat16)
    spread = pltpu.VMEM((fft * GROUP, inputs), jnp.float32)
    last, first = pl.pallas_call(
        tails_kernel,
        in_specs=[hbm],
        out_specs=[vmem, vmem],
        out_shape=[
            pltpu.VMEM((inputs, past), jnp.bfloat16),
            pltpu.VMEM((inputs, ahead), jnp.bfloat16),
        ],
        scratch_shapes=[
            pltpu.VMEM((inputs, past), jnp.int32),
            pltpu.VMEM((inputs, ahead), jnp.int32),
            pltpu.SemaphoreType.DMA((2,)),
        ],
        compiler_params=pltpu.CompilerParams(vmem_limit_bytes=8 << 20),
        name="tails",
    )(in_hbm(samples))
    from_behind = lax.ppermute(last, "tm", ring)
    from_ahead = lax.ppermute(first, "tm", [(b, a) for a, b in ring])

    spectra, partial = pl.pallas_call(
        own_kernel,
        in_specs=[hbm, hbm, hbm],
        out_specs=[vmem, vmem],
        out_shape=[spectra_type, pltpu.VMEM((GROUP, inputs, fft), jnp.float32)],
        scratch_shapes=[
            pltpu.VMEM((taps, fft), jnp.float32),
            pltpu.VMEM((fft, fft), jnp.bfloat16),
            pltpu.VMEM((inputs, sample_count), jnp.int32),
            [filt, filt],
            [spread, spread],
            pltpu.SemaphoreType.DMA((GROUP // 2 + groups,)),
        ],
        compiler_params=pltpu.CompilerParams(vmem_limit_bytes=24 << 20),
        name="own_frames",
    )(in_hbm(samples), in_hbm(coefficients), in_hbm(table))
    spectra = pl.pallas_call(
        functools.partial(edge_kernel, frames=frames),
        in_specs=[smem] * 2 + [vmem] * 6,
        out_specs=vmem,
        out_shape=spectra_type,
        scratch_shapes=[
            pltpu.VMEM((taps, fft), jnp.float32),
            filt,
            spread,
        ],
        input_output_aliases={7: 0},
        compiler_params=pltpu.CompilerParams(vmem_limit_bytes=16 << 20),
        name="edge_frames",
    )(has_behind, has_own, from_behind, from_ahead, partial, coefficients, table, spectra)

    items = fft // (2 * devices)
    outgoing = spectra.reshape(devices, 2 * items, frames, inputs)
    received = lax.all_to_all(outgoing, ("tm", "input"), 0, 0, tiled=True)
    received = received.reshape(tm_count, input_count, items, 2, frames, inputs)
    depth = 2 * tm_count * frames
    width = input_count * inputs
    blocks = (width // BLOCK) ** 2
    return pl.pallas_call(
        correlate_kernel,
        in_specs=[vmem],
        out_specs=hbm,
        out_shape=jax.ShapeDtypeStruct((items, 2, width, width), jnp.bfloat16),
        scratch_shapes=[
            pltpu.VMEM((items, depth, width), jnp.bfloat16),
            pltpu.VMEM((items, width, depth), jnp.bfloat16),
            pltpu.VMEM((items, depth, width), jnp.bfloat16),
            pltpu.VMEM((items, 2, width, width), jnp.bfloat16),
            pltpu.SemaphoreType.DMA((2 * items * blocks,)),
        ],
        compiler_params=pltpu.CompilerParams(vmem_limit_bytes=36 << 20),
        name="correlate",
    )(received)


def solution(mesh):
    in_specs = (P("input", "tm"), P())
    out_specs = P(("tm", "input"), None, None, None)
    return jax.shard_map(local, mesh=mesh, in_specs=in_specs, out_specs=out_specs, check_vma=False)
```

```python
import functools

import jax
import jax.numpy as jnp
import ml_dtypes
import numpy as np
from jax import lax
from jax.experimental import pallas as pl
from jax.experimental.pallas import tpu as pltpu
from jax.sharding import PartitionSpec as P

GROUP = 8
BLOCK = 256
ROWS = 16
LANES = 128
AHEAD = 2


def dft_table(length):
    channel = np.arange(length) // 2
    phase = channel[:, None] * np.arange(length)[None, :] % length
    angles = phase * (2.0 * np.pi / length)
    real = (np.arange(length) % 2 == 0)[:, None]
    values = np.where(real, np.cos(angles), -np.sin(angles)) / np.sqrt(length)
    return (values.astype(ml_dtypes.bfloat16).astype(np.float32) / 8.0).astype(ml_dtypes.bfloat16)


def edge_frames(frames):
    return [*range(AHEAD, GROUP), *range(frames, frames + AHEAD)]


def tails_kernel(samples_ref, last_ref, first_ref, last, first, sems):
    count = samples_ref.shape[1]
    copies = [
        pltpu.make_async_copy(
            samples_ref.at[:, pl.ds(count - last.shape[1], last.shape[1])], last, sems.at[0]
        ),
        pltpu.make_async_copy(samples_ref.at[:, pl.ds(0, first.shape[1])], first, sems.at[1]),
    ]
    for copy in copies:
        copy.start()
    for copy, source, target in zip(copies, (last, first), (last_ref, first_ref), strict=True):
        copy.wait()
        target[...] = source[...].astype(jnp.float32).astype(jnp.bfloat16)


def transform_pair(filt, f, table_ref, spread):
    frames, inputs, fft = filt.shape
    pair = filt[f : f + 2].reshape(2 * inputs, fft)
    spectra = lax.dot_general(
        table_ref[...], pair, (((1,), (1,)), ((), ())), preferred_element_type=jnp.float32
    )
    spread[pl.ds(f, fft, stride=frames), :] = spectra[:, :inputs]
    spread[pl.ds(f + 1, fft, stride=frames), :] = spectra[:, inputs:]


def pack(spread, spectra_ref, group, part, parts):
    rows, _, inputs = spectra_ref.shape
    count = rows // parts
    block = spread[part * count * GROUP : (part + 1) * count * GROUP, :]
    where = (slice(part * count, (part + 1) * count), slice(group * GROUP, (group + 1) * GROUP))
    spectra_ref[where] = block.reshape(count, GROUP, inputs).astype(jnp.bfloat16)


def own_kernel(
    samples_ref, coef_hbm, table_hbm, spectra_ref, partial_ref,
    coef_ref, table_ref, held, filts, spreads, sems,
):
    taps, fft = coef_ref.shape
    inputs, count = held.shape
    frames = count // fft
    groups = frames // GROUP
    span = GROUP * fft
    edge = edge_frames(frames)
    pairs = GROUP // 2
    chunk = inputs // pairs

    boxes = [(slice(k * chunk, (k + 1) * chunk), slice(0, 2 * span)) for k in range(pairs)]
    boxes += [(slice(0, inputs), slice(g * span, (g + 1) * span)) for g in range(2, groups)]
    loads = [
        pltpu.make_async_copy(
            samples_ref.at[pl.ds(r.start, r.stop - r.start), pl.ds(c.start, c.stop - c.start)],
            held.at[pl.ds(r.start, r.stop - r.start), pl.ds(c.start, c.stop - c.start)],
            sems.at[k],
        )
        for k, (r, c) in enumerate(boxes)
    ]
    coef_copy = pltpu.make_async_copy(coef_hbm, coef_ref, sems.at[len(loads)])
    table_copy = pltpu.make_async_copy(table_hbm, table_ref, sems.at[len(loads) + 1])
    coef_copy.start()
    for load in loads[:3]:
        load.start()
    table_copy.start()

    def arrive(k):
        loads[k].wait()
        if k + 3 < len(loads):
            loads[k + 3].start()

    def filter_rows(g, i):
        rows = slice(i, i + ROWS)
        for n in range(0, fft, LANES):
            coefs = [coef_ref[p : p + 1, n : n + LANES] for p in range(taps)]

            def frame(f):
                return held[rows, f * fft + n : f * fft + n + LANES].astype(jnp.float32)

            def share(f, known):
                total = None
                for p in range(taps):
                    if f - p in known:
                        term = coefs[p] * known[f - p]
                        total = term if total is None else total + term
                return total

            if g == 0:
                known = {f: frame(f) for f in range(GROUP)}
                for slot, f in enumerate(edge[:-AHEAD]):
                    partial_ref[slot, rows, n : n + LANES] = share(f, known)
                known = {f: frame(f) for f in range(frames + 1 - taps, frames)}
                for slot, f in enumerate(edge[-AHEAD:]):
                    partial_ref[slot + GROUP - AHEAD, rows, n : n + LANES] = share(f, known)
            else:
                known = {f: frame(f) for f in range(g * GROUP + 1 - taps, g * GROUP)}
                for slot in range(GROUP):
                    f = g * GROUP + slot
                    known[f] = frame(f)
                    filts[g % 2][slot, rows, n : n + LANES] = share(f, known).astype(jnp.bfloat16)

    coef_copy.wait()
    for g in range(1, groups):
        if g == 2:
            table_copy.wait()
        if g >= 2:
            arrive(pairs + g - 2)
        for pair in range(pairs):
            if g >= 2:
                transform_pair(filts[(g - 1) % 2], 2 * pair, table_ref, spreads[(g - 1) % 2])
            if g >= 3:
                pack(spreads[g % 2], spectra_ref, g - 2, pair, pairs)
            if g == 1:
                arrive(pair)
            for i in range(pair * chunk, (pair + 1) * chunk, ROWS):
                filter_rows(g, i)
    last = groups - 1
    for pair in range(pairs):
        transform_pair(filts[last % 2], 2 * pair, table_ref, spreads[last % 2])
        pack(spreads[(last - 1) % 2], spectra_ref, last - 1, pair, pairs)
        filter_rows(0, pair * 2 * ROWS)
        filter_rows(0, pair * 2 * ROWS + ROWS)
    pack(spreads[last % 2], spectra_ref, last, 0, 1)


def edge_kernel(
    has_behind_ref, has_own_ref, behind_ref, ahead_ref, partial_ref, coef_ref, table_ref, _, spectra_ref,
    masked_ref, filt, spread, *, frames,
):
    taps, fft = coef_ref.shape
    inputs = behind_ref.shape[0]
    past = behind_ref.shape[1] // fft
    has_own = has_own_ref[0]
    edge = edge_frames(frames)
    masked_ref[...] = coef_ref[...] * has_behind_ref[0]

    for slot in range(0, GROUP, 2):
        for i in range(0, inputs, ROWS):
            rows = slice(i, i + ROWS)
            for n in range(0, fft, LANES):
                lanes = slice(n, n + LANES)
                samples = {}

                def frame(f):
                    if f not in samples:
                        ref, k = (behind_ref, f + past) if f < 0 else (ahead_ref, f - frames)
                        value = ref[rows, k * fft + n : k * fft + n + LANES]
                        samples[f] = value.astype(jnp.float32)
                    return samples[f]

                for s in (slot, slot + 1):
                    f = edge[s]
                    value = partial_ref[s, rows, lanes]
                    if f < frames:
                        for p in range(f + 1, taps):
                            value = value + masked_ref[p : p + 1, lanes] * frame(f - p)
                    else:
                        value = value * has_own
                        for p in range(f - frames + 1):
                            value = value + coef_ref[p : p + 1, lanes] * frame(f - p)
                    filt[s, rows, lanes] = value.astype(jnp.bfloat16)
        transform_pair(filt, slot, table_ref, spread)
    pack(spread, spectra_ref, 0, 0, 1)


def correlate_kernel(recv_ref, out_ref, held, turned, swapped, stage, sems):
    tm_count, input_count, items, _, frames, inputs = recv_ref.shape
    half = tm_count * frames
    width = input_count * inputs
    scale = 1.0 / half
    copies = []

    def give(c, part, i, j, value):
        rows, cols = pl.ds(i, BLOCK), pl.ds(j, BLOCK)
        stage[c, part, rows, cols] = value
        copy = pltpu.make_async_copy(
            stage.at[c, part, rows, cols], out_ref.at[c, part, rows, cols], sems.at[len(copies)]
        )
        copy.start()
        copies.append(copy)

    for c in range(items):
        for r in range(2):
            for a in range(tm_count):
                for b in range(input_count):
                    rows = slice(r * half + a * frames, r * half + (a + 1) * frames)
                    cols = slice(b * inputs, (b + 1) * inputs)
                    held[c, rows, cols] = recv_ref[a, b, c, r]
        turned[c] = held[c].T
        swapped[c, :half] = -held[c, half:]
        swapped[c, half:] = held[c, :half]
        for i in range(0, width, BLOCK):
            for j in range(i, width, BLOCK):
                left = turned[c, i : i + BLOCK]
                real = scale * jnp.dot(
                    left, held[c, :, j : j + BLOCK], preferred_element_type=jnp.float32
                )
                if j > i:
                    imag = scale * jnp.dot(
                        left, swapped[c, :, j : j + BLOCK], preferred_element_type=jnp.float32
                    )
                else:
                    cross = scale * jnp.dot(
                        turned[c, i : i + BLOCK, half:],
                        held[c, :half, j : j + BLOCK],
                        preferred_element_type=jnp.float32,
                    )
                    imag = cross - cross.T
                real = real.astype(jnp.bfloat16)
                imag = imag.astype(jnp.bfloat16)
                give(c, 0, i, j, real)
                give(c, 1, i, j, imag)
                if j > i:
                    give(c, 0, j, i, real.T)
                    give(c, 1, j, i, (-imag).T)
    for copy in copies:
        copy.wait()


def local(samples, coefficients):
    inputs, sample_count = samples.shape
    taps, fft = coefficients.shape
    frames = sample_count // fft
    tm_count = lax.axis_size("tm")
    input_count = lax.axis_size("input")
    devices = tm_count * input_count
    groups = frames // GROUP
    past = (taps - 1 - AHEAD) * fft
    ahead = AHEAD * fft
    table = jnp.asarray(dft_table(fft))
    vmem = pl.BlockSpec(memory_space=pltpu.VMEM)
    smem = pl.BlockSpec(memory_space=pltpu.SMEM)
    hbm = pl.BlockSpec(memory_space=pltpu.HBM)

    ring = [(i, (i + 1) % tm_count) for i in range(tm_count)]
    own_tm = lax.axis_index("tm")
    has_behind = jnp.where(own_tm > 0, 1.0, 0.0).astype(jnp.float32).reshape(1)
    has_own = jnp.where(own_tm < tm_count - 1, 1.0, 0.0).astype(jnp.float32).reshape(1)
    spectra_type = pltpu.VMEM((fft, frames, inputs), jnp.bfloat16)
    in_hbm = lambda array: pltpu.with_memory_space_constraint(array, pltpu.HBM)
    filt = pltpu.VMEM((GROUP, inputs, fft), jnp.bfloat16)
    spread = pltpu.VMEM((fft * GROUP, inputs), jnp.float32)
    last, first = pl.pallas_call(
        tails_kernel,
        in_specs=[hbm],
        out_specs=[vmem, vmem],
        out_shape=[
            pltpu.VMEM((inputs, past), jnp.bfloat16),
            pltpu.VMEM((inputs, ahead), jnp.bfloat16),
        ],
        scratch_shapes=[
            pltpu.VMEM((inputs, past), jnp.int32),
            pltpu.VMEM((inputs, ahead), jnp.int32),
            pltpu.SemaphoreType.DMA((2,)),
        ],
        compiler_params=pltpu.CompilerParams(vmem_limit_bytes=8 << 20),
        name="tails",
    )(in_hbm(samples))
    from_behind = lax.ppermute(last, "tm", ring)
    from_ahead = lax.ppermute(first, "tm", [(b, a) for a, b in ring])

    spectra, partial = pl.pallas_call(
        own_kernel,
        in_specs=[hbm, hbm, hbm],
        out_specs=[vmem, vmem],
        out_shape=[spectra_type, pltpu.VMEM((GROUP, inputs, fft), jnp.float32)],
        scratch_shapes=[
            pltpu.VMEM((taps, fft), jnp.float32),
            pltpu.VMEM((fft, fft), jnp.bfloat16),
            pltpu.VMEM((inputs, sample_count), jnp.int32),
            [filt, filt],
            [spread, spread],
            pltpu.SemaphoreType.DMA((GROUP // 2 + groups,)),
        ],
        compiler_params=pltpu.CompilerParams(vmem_limit_bytes=24 << 20),
        name="own_frames",
    )(in_hbm(samples), in_hbm(coefficients), in_hbm(table))
    spectra = pl.pallas_call(
        functools.partial(edge_kernel, frames=frames),
        in_specs=[smem] * 2 + [vmem] * 6,
        out_specs=vmem,
        out_shape=spectra_type,
        scratch_shapes=[
            pltpu.VMEM((taps, fft), jnp.float32),
            filt,
            spread,
        ],
        input_output_aliases={7: 0},
        compiler_params=pltpu.CompilerParams(vmem_limit_bytes=16 << 20),
        name="edge_frames",
    )(has_behind, has_own, from_behind, from_ahead, partial, coefficients, table, spectra)

    items = fft // (2 * devices)
    outgoing = spectra.reshape(devices, 2 * items, frames, inputs)
    received = lax.all_to_all(outgoing, ("tm", "input"), 0, 0, tiled=True)
    received = received.reshape(tm_count, input_count, items, 2, frames, inputs)
    depth = 2 * tm_count * frames
    width = input_count * inputs
    blocks = (width // BLOCK) ** 2
    return pl.pallas_call(
        correlate_kernel,
        in_specs=[vmem],
        out_specs=hbm,
        out_shape=jax.ShapeDtypeStruct((items, 2, width, width), jnp.bfloat16),
        scratch_shapes=[
            pltpu.VMEM((items, depth, width), jnp.bfloat16),
            pltpu.VMEM((items, width, depth), jnp.bfloat16),
            pltpu.VMEM((items, depth, width), jnp.bfloat16),
            pltpu.VMEM((items, 2, width, width), jnp.bfloat16),
            pltpu.SemaphoreType.DMA((2 * items * blocks,)),
        ],
        compiler_params=pltpu.CompilerParams(vmem_limit_bytes=36 << 20),
        name="correlate",
    )(received)


def solution(mesh):
    in_specs = (P("input", "tm"), P())
    out_specs = P(("tm", "input"), None, None, None)
    return jax.shard_map(local, mesh=mesh, in_specs=in_specs, out_specs=out_specs, check_vma=False)
```
